32 devices in a mesh: gx: 8 (over z, x), gy: 4 (over y, core).
Axes of the slice: x: 2, y: 2, z: 4, core: 2. Of those that a mesh axis runs over, the one named last changes fastest.
Arguments:
- right_side: float32 [128, 128, 128], P('gx', 'gy'), may hold values from -13 to 13
- accumulation: float32 [128, 128, 128], P('gx', 'gy'), may hold values from 0.05 to 0.5
- trans_x: float32 [128, 128, 128], P('gx', 'gy'), may hold values from 0.1 to 2
- trans_y: float32 [128, 128, 128], P('gx', 'gy'), may hold values from 0.1 to 2
- trans_z: float32 [128, 128, 128], P('gx', 'gy'), may hold values from 0.1 to 2
- perf_cells: int32 [512, 256], P(('gx', 'gy')), may hold values from 0 to 65535
- perf_live: int32 [512, 256], P(('gx', 'gy')), may hold values 0 or 1
- well_region: int32 [512, 1], P(('gx', 'gy')), may hold values from 0 to 7; in each aligned block of 16 rows (0 to 15, 16 to 31, ...) at most 2 rows name the same one
- schur_blocks: float32 [512, 256, 256], P(('gx', 'gy')), may hold values from -8 to 10, as said below
Outputs:
- pressure_update: float32 [128, 128, 128], P('gx', 'gy')
- residual: float32 [128, 128, 128], P('gx', 'gy')
The draws below stay inside these ranges and needn't reach their ends.
Inputs may be any that keep to these rules, and one draw needn't show every extreme that they name: `perf_cells`: well w is owned by the device at position w // 16 of gx+gy; its slot's cell is a flat index (x slowest, layer fastest) within the block of 16 x 32 x 128 cells of the device at x index well_region[w] and at the owner's y index. `well_region`: among the wells of one owner, no x index is named more than 2 times, and some x index exactly 2 times. `schur_blocks`: each block is symmetric positive definite.
All inputs are finite; a program needn't handle non-finite values. No bound on the sum of `perf_live` on one device may be relied on, other than what follows from the above.
Results may differ from the reference program's by a relative error of at most 0.0003.
Values sent between devices are 32-bit elements; how exact they have to be, the bound alone decides.
A program may use at most 64 MiB of HBM per device.

```python
import math
import jax
import jax.numpy as jnp
import numpy as np
from jax import lax

CX = 16
CY = 32
NZ = 128
WELL_DEV = 16
PERF = 256
WCAP = 2
ITERS = 6
NX = 128
NY = 128
WELLS = 512
N_GX = 8
N_GY = 4


def draw_right_side(key, part):
    key_noise = jax.random.fold_in(key, 11)
    pos_x = jnp.arange(NX, dtype=jnp.float32) / max(NX - 1, 1)
    pos_y = jnp.arange(NY, dtype=jnp.float32) / max(NY - 1, 1)
    scaling = jnp.exp(math.log(3.0) * (pos_x[:, None] + pos_y[None, :] - 1.0))[:, :, None]
    noise = jnp.clip(jax.random.normal(key_noise, (NX, NY, NZ), jnp.float32), -4.0, 4.0)
    return noise * scaling


def draw_schur_blocks(key, part):
    key_factor = jax.random.fold_in(key, 21)
    key_spread = jax.random.fold_in(key, 22)
    factor = jnp.clip(jax.random.normal(key_factor, (WELLS, PERF, PERF), jnp.float32), -4.0, 4.0)
    spread = jnp.exp(jax.random.uniform(key_spread, (WELLS, PERF), jnp.float32, math.log(0.5), math.log(2.0)))
    product = jnp.einsum('wik,wjk->wij', factor, factor) * (0.5 / PERF)
    eye_block = jnp.eye(PERF, dtype=jnp.float32)[None, :, :]
    return product + eye_block * spread[:, :, None]


def with_ends(array, rng, smallest, top_value):
    shape = array.shape
    spot = [jax.random.randint(jax.random.fold_in(rng, axis), (), 0, shape[axis]) for axis in range(len(shape))]
    array = array.at[tuple(spot)].set(smallest)
    longest = shape.index(max(shape))
    spot[longest] = (spot[longest] + 1) % shape[longest]
    return array.at[tuple(spot)].set(top_value)


def block_levels(stream_key, shape, split, least, top_value):
    factor_of, own = 1.0, jax.random.fold_in(stream_key, 6)
    for axis_at, blocks in split:
        steps = jnp.exp(jax.random.uniform(jax.random.fold_in(own, axis_at), (blocks,), jnp.float32, least / len(split), top_value / len(split)))
        factor_of = factor_of * jnp.repeat(steps, shape[axis_at] // blocks).reshape([-1 if axis == axis_at else 1 for axis in range(len(shape))])
    return factor_of


def assign_block(rng, own, number, rows, amount, top, most, lean):
    sequence = jax.random.permutation(rng, amount)
    heavy_load, ordinary = shares(amount, rows * top, most, lean, True), shares(amount, rows * top, most, lean, False)
    places = jnp.arange(amount)

    def named(sizes, turn):
        used = int((sizes > 0).sum())
        fixed = max(1, used // 4)
        moved = fixed + (places - fixed + turn * (used - fixed)) % max(1, amount - fixed)
        return jnp.zeros((amount,), jnp.int32).at[sequence[jnp.where(places < fixed, places, moved)]].set(jnp.asarray(sizes, jnp.int32))

    sizes = jnp.where(number % 4 == 0, named(heavy_load, number // 4), named(ordinary, number - number // 4 - 1))
    mixed = jax.random.permutation(jax.random.fold_in(own, 3), amount)
    giver, taker = mixed[0:amount // 2 * 2:2], mixed[1:amount // 2 * 2:2]
    margin = jnp.minimum(sizes[giver] - 1, most - sizes[taker]) // 2
    margin = jnp.where((giver == sequence[0]) | (taker == sequence[0]) | (sizes[taker] == 0), 0, jnp.maximum(margin, 0))
    moved = jax.random.randint(jax.random.fold_in(own, 4), (amount // 2,), 0, 1 << 20) % (margin + 1)
    sizes = sizes.at[giver].add(-moved).at[taker].add(moved)
    members = jnp.searchsorted(jnp.cumsum(sizes), jnp.arange(rows * top), side="right").astype(jnp.int32)
    table = members.reshape(top, rows).T
    table = table[jax.random.permutation(jax.random.fold_in(own, 1), rows)]
    turn = jax.random.randint(jax.random.fold_in(own, 2), (rows, 1), 0, top)
    return jnp.take_along_axis(table, (jnp.arange(top)[None, :] + turn) % top, axis=1)


def shares(amount, total, reach, lean, full):
    loads = [(1 << 20) // math.isqrt(grade ** lean) + 1 for grade in range(1, amount + 1)]
    largest = reach if full else min(reach, max(-(-total // amount), total * loads[0] // sum(loads)))
    least = 1 if total - largest >= amount - 1 else 0
    given, surplus = [largest] + [least] * (amount - 1), total - largest - least * (amount - 1)
    while surplus > 0:
        free = [i for i in range(1, amount) if given[i] < largest] or [i for i in range(1, amount) if given[i] < reach]
        mass, remaining = sum([loads[i] for i in free]), surplus
        for i in free:
            extra = min(reach - given[i], max(1, remaining * loads[i] // mass), surplus)
            given[i] = given[i] + extra
            surplus = surplus - extra
    return np.array(given)


def setup_inputs(seed: int = 0) -> dict:
    key_list = jax.random.split(jax.random.key(seed), 10)
    right_side = draw_right_side(jax.random.fold_in(key_list[9], 71), 0)
    accumulation = jnp.clip(jnp.exp(math.log(0.5) - 2.3025851 * jax.random.uniform(key_list[1], (NX, NY, NZ), jnp.float32) ** block_levels(key_list[1], (NX, NY, NZ), ((0, 8), (1, 4)), -0.2, 0.2)), 0.05, 0.5)
    trans_x = jnp.clip(jnp.exp(math.log(2.0) - 2.9957323 * jax.random.uniform(key_list[2], (NX, NY, NZ), jnp.float32) ** block_levels(key_list[2], (NX, NY, NZ), ((0, 8), (1, 4)), -0.2, 0.2)), 0.1, 2.0)
    trans_y = jnp.clip(jnp.exp(math.log(2.0) - 2.9957323 * jax.random.uniform(key_list[3], (NX, NY, NZ), jnp.float32) ** block_levels(key_list[3], (NX, NY, NZ), ((0, 8), (1, 4)), -0.2, 0.2)), 0.1, 2.0)
    trans_z = jnp.clip(jnp.exp(math.log(2.0) - 2.9957323 * jax.random.uniform(key_list[4], (NX, NY, NZ), jnp.float32) ** block_levels(key_list[4], (NX, NY, NZ), ((0, 8), (1, 4)), -0.2, 0.2)), 0.1, 2.0)
    perf_cells = with_ends(jax.random.randint(key_list[5], (WELLS, PERF), 0, CX * CY * NZ), jax.random.fold_in(key_list[5], 1), 0, (CX * CY * NZ) - 1).astype(jnp.int32)
    perf_live = with_ends((jax.random.randint(key_list[6], (WELLS, PERF), 0, 4) < 3).astype(jnp.int32), jax.random.fold_in(key_list[6], 1), 0, 1)
    well_region_keys = jax.random.split(jax.random.fold_in(key_list[7], 1), WELLS // WELL_DEV)
    well_region_turns = jax.random.permutation(jax.random.fold_in(key_list[7], 3), WELLS // WELL_DEV)
    well_region = jax.vmap(lambda own, number: assign_block(jax.random.fold_in(key_list[7], 2), own, number, WELL_DEV, N_GX, 1, WCAP, 2))(well_region_keys, well_region_turns).reshape((WELLS, 1))
    schur_blocks = draw_schur_blocks(jax.random.fold_in(key_list[9], 71), 0)
    return dict(right_side=right_side, accumulation=accumulation, trans_x=trans_x, trans_y=trans_y, trans_z=trans_z, perf_cells=perf_cells, perf_live=perf_live, well_region=well_region, schur_blocks=schur_blocks)


def shifted_prev(values, axis_number):
    widths = [(0, 0), (0, 0), (0, 0)]
    widths[axis_number] = (1, 0)
    padded = jnp.pad(values, widths)
    return lax.slice_in_dim(padded, 0, values.shape[axis_number], axis=axis_number)


def shifted_next(values, axis_number):
    widths = [(0, 0), (0, 0), (0, 0)]
    widths[axis_number] = (0, 1)
    padded = jnp.pad(values, widths)
    return lax.slice_in_dim(padded, 1, values.shape[axis_number] + 1, axis=axis_number)


def perforation_index(perf_cells, well_region):
    wells_total = perf_cells.shape[0]
    owners = jnp.arange(wells_total, dtype=jnp.int32) // WELL_DEV
    owner_y = owners % N_GY
    region = well_region[:, 0]
    layer_x = perf_cells // (CY * NZ)
    layer_y = (perf_cells // NZ) % CY
    layer_z = perf_cells % NZ
    glob_x = region[:, None] * CX + layer_x
    glob_y = owner_y[:, None] * CY + layer_y
    return ((glob_x * NY + glob_y) * NZ + layer_z).astype(jnp.int32)


def well_term(field, cell_index, live_mask, schur_blocks):
    picked = field.reshape(-1)[cell_index] * live_mask
    pushed = jnp.einsum("wij,wj->wi", schur_blocks, picked, precision=lax.Precision.HIGHEST) * live_mask
    flat = jnp.zeros((field.size,), field.dtype).at[cell_index.reshape(-1)].add(pushed.reshape(-1))
    return flat.reshape(field.shape)


def reference(right_side, accumulation, trans_x, trans_y, trans_z, perf_cells, perf_live, well_region, schur_blocks):
    face_x = trans_x.at[-1].set(0.0)
    face_y = trans_y.at[:, -1].set(0.0)
    face_z = trans_z.at[:, :, -1].set(0.0)
    prev_x = shifted_prev(face_x, 0)
    prev_y = shifted_prev(face_y, 1)
    prev_z = shifted_prev(face_z, 2)
    diagonal = accumulation + face_x + prev_x + face_y + prev_y + face_z + prev_z
    cell_index = perforation_index(perf_cells, well_region)
    live_mask = perf_live.astype(right_side.dtype)

    def operate(field):
        local_part = (accumulation * field
                      + face_x * (field - shifted_next(field, 0)) + prev_x * (field - shifted_prev(field, 0))
                      + face_y * (field - shifted_next(field, 1)) + prev_y * (field - shifted_prev(field, 1))
                      + face_z * (field - shifted_next(field, 2)) + prev_z * (field - shifted_prev(field, 2)))
        return local_part + well_term(field, cell_index, live_mask, schur_blocks)

    solution = jnp.zeros_like(right_side)
    residual = right_side
    precon = residual / diagonal
    direction = precon
    product_now = jnp.sum(residual * precon)
    for counter in range(ITERS):
        applied = operate(direction)
        step_size = product_now / jnp.sum(direction * applied)
        solution = solution + step_size * direction
        residual = residual - step_size * applied
        precon = residual / diagonal
        product_next = jnp.sum(residual * precon)
        direction = precon + (product_next / product_now) * direction
        product_now = product_next
    return solution, residual
```

```python
import functools

import jax
import jax.numpy as jnp
from jax import lax
from jax.experimental import pallas as pl
from jax.experimental.pallas import tpu as pltpu
from jax.sharding import PartitionSpec as P

WCAP = 2
ITERS = 6
MESH = pl.DeviceIdType.MESH


def split_bf16(values):
    high = values.astype(jnp.bfloat16).astype(jnp.float32)
    return high, values - high


def kernel(
    n,
    ny,
    rows_x,
    rows_y,
    region_ref,
    rhs_hbm,
    acc_hbm,
    tx_hbm,
    ty_hbm,
    tz_hbm,
    cells_ref,
    live_ref,
    schur_hbm,
    x_ref,
    r_ref,
    rhs_ref,
    acc_ref,
    tx_ref,
    ty_ref,
    tz_ref,
    schur_vm,
    schur_out,
    schur_in,
    schur_two,
    onehot,
    vl_ref,
    lay_ref,
    req_send,
    req_recv,
    send_b,
    recv_b,
    send_c,
    recv_c,
    send_g,
    recv_g,
    ysend,
    xrecv,
    yrecv,
    yface_send,
    xface_recv,
    yface_recv,
    fx_ref,
    fy_ref,
    py_ref,
    fz_ref,
    pz_ref,
    inv_ref,
    m_ref,
    w_ref,
    z_ref,
    p_ref,
    s_ref,
    nloc_ref,
    dots_ref,
    local_sem,
    field_sem,
    schur_ss,
    schur_rs,
    req_ss,
    req_rs,
    face_ss,
    face_rs,
    halo_ss,
    halo_rs,
    b_ss,
    b_rs,
    c_ss,
    c_rs,
    g_ss,
    g_rs,
):
    cols, layers = rhs_ref.shape
    wells, perf = cells_ref.shape
    chunk = WCAP * perf
    shift = layers.bit_length() - 1
    assert layers == 1 << shift and n == 1 << (n.bit_length() - 1)
    me, my = lax.axis_index("gx"), lax.axis_index("gy")

    def across(d):
        peer = me
        for bit in range(n.bit_length() - 1):
            if d >> bit & 1:
                peer = peer + (1 << bit) * (1 - 2 * lax.rem(lax.div(me, 1 << bit), 2))
        return peer

    def at_peer(d):
        return {"gx": across(d)}

    def at_x(d):
        return {"gx": lax.rem(me + (d + n), n)}

    def at_y(d):
        return {"gy": lax.rem(my + (d + ny), ny)}

    def at_other():
        return {"gy": my + 1 - 2 * lax.rem(my, 2)}

    def at_cross(d):
        return {"gx": across(d), **at_other()}

    def remote(src, dst, ss, rs, where):
        return pltpu.make_async_remote_copy(
            src_ref=src, dst_ref=dst, send_sem=ss, recv_sem=rs, device_id=where, device_id_type=MESH
        )

    schur_copy = pltpu.make_async_copy(schur_hbm, schur_vm, local_sem)
    loads = [
        pltpu.make_async_copy(src, dst, field_sem.at[i])
        for i, (src, dst) in enumerate(
            (
                (ty_hbm, ty_ref),
                (tx_hbm, tx_ref),
                (tz_hbm, tz_ref),
                (acc_hbm, acc_ref),
                (rhs_hbm, rhs_ref),
            )
        )
    ]
    for copy in loads:
        copy.start()
    schur_copy.start()
    xrecv[...] = jnp.zeros_like(xrecv)
    barrier = pltpu.get_barrier_semaphore()
    for d in range(1, n):
        pl.semaphore_signal(barrier, inc=1, device_id=at_peer(d), device_id_type=MESH)
    for d in range(1, ny):
        pl.semaphore_signal(barrier, inc=1, device_id=at_y(d), device_id_type=MESH)
    for d in range(1, n):
        pl.semaphore_signal(barrier, inc=1, device_id=at_cross(d), device_id_type=MESH)

    well_at = []
    for d in range(n):
        peer = across(d)
        found = [jnp.int32(0)] * WCAP
        count = jnp.int32(0)
        for w in range(wells):
            match = region_ref[0, w] == peer
            for j in range(WCAP):
                found[j] = jnp.where(jnp.logical_and(match, count == j), jnp.int32(w), found[j])
            count = count + match.astype(jnp.int32)
        well_at.append(found)
        target = req_send if d else req_recv
        for j in range(WCAP):
            used = (count > j).astype(jnp.int32)
            span = slice(j * perf, (j + 1) * perf)
            open_slot = live_ref[pl.ds(found[j], 1), :] * used
            target[d, :, span] = (cells_ref[pl.ds(found[j], 1), :] + 1) * open_slot - 1
    loads[0].wait()
    loads[1].wait()
    yface_send[...] = ty_ref[pl.ds(rows_y - 1, rows_x, stride=rows_y), :]

    pl.semaphore_wait(barrier, 2 * (n - 1) + ny - 1)
    requests = [
        remote(req_send.at[d], req_recv.at[d], req_ss.at[d], req_rs.at[d], at_peer(d)) for d in range(1, n)
    ]
    face_out = [
        remote(
            tx_ref.at[pl.ds(cols - rows_y, rows_y)], xface_recv, face_ss.at[0], face_rs.at[0], at_x(1)
        ),
        remote(yface_send, yface_recv, face_ss.at[1], face_rs.at[1], at_y(1)),
    ]
    for copy in requests[::-1] + face_out:
        copy.start()

    edges = [n, n - 1]
    while edges[-1] > 3:
        edges.append(edges[-1] - 2)
    edges.append(0)
    ranges = [range(low, high) for high, low in zip(edges[:-1], edges[1:])]
    swaps = [
        remote(
            schur_out.at[pl.ds(d * WCAP, WCAP)],
            schur_in.at[pl.ds(d * WCAP, WCAP)],
            schur_ss.at[d],
            schur_rs.at[d],
            at_other(),
        )
        for d in range(n)
    ]
    schur_copy.wait()
    for group in ranges:
        for d in group:
            for j in range(WCAP):
                schur_out[d * WCAP + j] = schur_vm[well_at[d][j]]
            swaps[d].start()

    last_x = me == n - 1
    last_y = my == ny - 1
    lane = lax.broadcasted_iota(jnp.int32, (rows_y, layers), 1)
    row = lax.broadcasted_iota(jnp.int32, (rows_y, layers), 0)
    zeros = jnp.zeros((rows_y, layers), jnp.float32)
    for copy in loads[2:]:
        copy.wait()
    for copy in face_out:
        copy.wait()
    fx_ref[0:rows_y, :] = jnp.where(me == 0, 0.0, xface_recv[...])
    for i in range(rows_x):
        at = slice(i * rows_y, (i + 1) * rows_y)
        after = slice((i + 1) * rows_y, (i + 2) * rows_y)
        fx = tx_ref[at, :]
        if i == rows_x - 1:
            fx = jnp.where(last_x, 0.0, fx)
        fx_ref[after, :] = fx
        fy = ty_ref[at, :]
        below = jnp.where(my == 0, 0.0, yface_recv[i : i + 1, :])
        py = jnp.where(row == 0, below, pltpu.roll(fy, 1, 0))
        fy = jnp.where(jnp.logical_and(last_y, row == rows_y - 1), 0.0, fy)
        fy_ref[at, :] = fy
        py_ref[at, :] = py
        fz = jnp.where(lane == layers - 1, 0.0, tz_ref[at, :])
        pz = pltpu.roll(fz, 1, 1)
        fz_ref[at, :] = fz
        pz_ref[at, :] = pz
        diagonal = acc_ref[at, :] + fx + fx_ref[at, :] + fy + py + fz + pz
        inverse = 1.0 / diagonal
        inv_ref[at, :] = inverse
        r = rhs_ref[at, :]
        r_ref[at, :] = r
        u = r * inverse
        m_ref[at, :] = u
        for ref in (x_ref, w_ref, z_ref, p_ref, s_ref):
            ref[at, :] = zeros
    dots_ref[...] = jnp.zeros_like(dots_ref)

    column = lax.broadcasted_iota(jnp.int32, (cols, chunk), 0)
    for d in range(n):
        if d:
            requests[d - 1].wait_recv()
        cells = req_recv[d]
        lay_ref[d] = jnp.bitwise_and(cells, layers - 1)
        onehot[:, d * chunk : (d + 1) * chunk] = (
            (column == lax.shift_right_logical(cells, shift)).astype(jnp.float32).astype(jnp.bfloat16)
        )
    for copy in requests:
        copy.wait_send()

    layer = lax.broadcasted_iota(jnp.int32, (layers, chunk), 0)
    pick_row = lax.broadcasted_iota(jnp.int32, (16, perf), 0)

    half = layers // 2
    first_half = lax.broadcasted_iota(jnp.int32, (1, layers), 1) < half

    def b_copy(par, d):
        return remote(send_b.at[par, d], recv_b.at[par, d], b_ss.at[par, d], b_rs.at[par, d], at_cross(d))

    def c_copy(par, d):
        return remote(send_c.at[par, d], recv_c.at[par, d], c_ss.at[par, d], c_rs.at[par, d], at_cross(d))

    def g_copy(par, d, slot):
        return remote(send_g.at[par], recv_g.at[par, slot], g_ss.at[par, d], g_rs.at[par, slot], at_y(d))

    def halo_copies(par):
        return [
            remote(
                m_ref.at[pl.ds(cols - rows_y, rows_y)],
                xrecv.at[par, 0],
                halo_ss.at[par, 0],
                halo_rs.at[par, 0],
                at_x(1),
            ),
            remote(
                m_ref.at[pl.ds(0, rows_y)], xrecv.at[par, 1], halo_ss.at[par, 1], halo_rs.at[par, 1], at_x(-1)
            ),
            remote(ysend.at[par, 0], yrecv.at[par, 0], halo_ss.at[par, 2], halo_rs.at[par, 2], at_y(1)),
            remote(ysend.at[par, 1], yrecv.at[par, 1], halo_ss.at[par, 3], halo_rs.at[par, 3], at_y(-1)),
        ]

    def start_sums(par):
        total = recv_b[par, 0, :, chunk:]
        for d in range(1, n):
            total = total + recv_b[par, d, :, chunk:]
        send_g[par] = total
        for d in range(1, ny):
            g_copy(par, d, ny - d).start()
        return total

    def end_sums(par, total):
        for d in range(1, ny):
            g_copy(par, d, d).wait_recv()
            total = total + recv_g[par, d]
        for d in range(1, ny):
            g_copy(par, d, d).wait_send()
        gam = jnp.sum(jnp.where(first_half, total, 0.0), axis=1, keepdims=True)
        dlt = jnp.sum(jnp.where(first_half, 0.0, total), axis=1, keepdims=True)
        return jnp.broadcast_to(gam, (1, layers)), jnp.broadcast_to(dlt, (1, layers))

    def start_halos(par):
        ysend[par, 0] = m_ref[pl.ds(rows_y - 1, rows_x, stride=rows_y), :]
        ysend[par, 1] = m_ref[pl.ds(0, rows_x, stride=rows_y), :]
        halos = halo_copies(par)
        pl.when(me < n - 1)(halos[0].start)
        pl.when(me > 0)(halos[1].start)
        for copy in halos[2:]:
            copy.start()

    def send_field(par):
        high, low = split_bf16(m_ref[...].T)
        lhs = jnp.concatenate([high, low], 0).astype(jnp.bfloat16)
        dots = dots_ref[...]
        for group in ranges:
            for d in group:
                part = jnp.dot(
                    lhs, onehot[:, d * chunk : (d + 1) * chunk], preferred_element_type=jnp.float32
                )
                part = part[:layers] + part[layers:]
                picked = jnp.sum(jnp.where(layer == lay_ref[d], part, 0.0), axis=0, keepdims=True)
                send_b[par, d, :, :chunk] = picked
                send_b[par, d, :, chunk:] = dots
            for d in group:
                b_copy(par, d).start()
            if group is ranges[0]:
                start_halos(par)

    def stencil(par):
        halos = halo_copies(par)
        x_up, x_down = halos[:2]

        @pl.when(me < n - 1)
        def _():
            x_up.wait_send()
            x_down.wait_recv()

        @pl.when(me > 0)
        def _():
            x_up.wait_recv()
            x_down.wait_send()

        for copy in halos[2:]:
            copy.wait()
        for i in range(rows_x):
            at = slice(i * rows_y, (i + 1) * rows_y)
            after = slice((i + 1) * rows_y, (i + 2) * rows_y)
            m = m_ref[at, :]
            below = m_ref[(i - 1) * rows_y : i * rows_y, :] if i else xrecv[par, 0]
            above = m_ref[after, :] if i < rows_x - 1 else xrecv[par, 1]
            y_prev = jnp.where(row == 0, yrecv[par, 0, i : i + 1, :], pltpu.roll(m, 1, 0))
            y_next = jnp.where(row == rows_y - 1, yrecv[par, 1, i : i + 1, :], pltpu.roll(m, rows_y - 1, 0))
            nloc_ref[at, :] = (
                acc_ref[at, :] * m
                + fx_ref[after, :] * (m - above)
                + fx_ref[at, :] * (m - below)
                + fy_ref[at, :] * (m - y_next)
                + py_ref[at, :] * (m - y_prev)
                + fz_ref[at, :] * (m - pltpu.roll(m, layers - 1, 1))
                + pz_ref[at, :] * (m - pltpu.roll(m, 1, 1))
            )

    def push(par):
        for group in ranges:
            for d in group:
                b_copy(par, d).wait_recv()
            for d in group:
                for j in range(WCAP):
                    span = slice(j * perf, (j + 1) * perf)
                    high, low = split_bf16(recv_b[par, d, :, span])
                    left = jnp.where(pick_row == 0, high, jnp.where(pick_row == 1, low, 0.0)).astype(
                        jnp.bfloat16
                    )
                    pushed = jnp.dot(
                        jnp.concatenate([left, left], 1),
                        schur_two[d * WCAP + j],
                        preferred_element_type=jnp.float32,
                    )
                    send_c[par, d, :, span] = jnp.sum(pushed, axis=0, keepdims=True)
            for d in group:
                c_copy(par, d).start()

    def scatter(par, group):
        for d in group:
            c_copy(par, d).wait_recv()
        for d in group:
            high, low = split_bf16(recv_c[par, d])
            here = layer == lay_ref[d]
            span = slice(d * chunk, (d + 1) * chunk)
            vl_ref[0:layers, span] = jnp.where(here, high, 0.0).astype(jnp.bfloat16)
            vl_ref[layers : 2 * layers, span] = jnp.where(here, low, 0.0).astype(jnp.bfloat16)
        span = slice(group[0] * chunk, (group[-1] + 1) * chunk)
        return lax.dot_general(
            onehot[:, span],
            vl_ref[:, span],
            (((1,), (1,)), ((), ())),
            preferred_element_type=jnp.float32,
        )

    def step(k, carried):
        gam_old, a_old = carried
        par = lax.rem(k, 2)
        send_field(par)
        stencil(par)
        push(par)
        total = start_sums(par)
        for d in range(n):
            b_copy(par, d).wait_send()
        gam, dlt = end_sums(par, total)
        b = jnp.where(k <= 1, 0.0, gam / gam_old)
        a = jnp.where(k == 0, 0.0, jnp.where(k == 1, gam / dlt, gam / (dlt - b * gam / a_old)))
        a_w = jnp.where(k == 0, -1.0, a)
        gamma = jnp.zeros((8, layers), jnp.float32)
        for i in range(rows_x):
            at = slice(i * rows_y, (i + 1) * rows_y)
            inverse = inv_ref[at, :]
            r = r_ref[at, :]
            p = r * inverse + b * p_ref[at, :]
            s = w_ref[at, :] + b * s_ref[at, :]
            p_ref[at, :] = p
            s_ref[at, :] = s
            x_ref[at, :] = x_ref[at, :] + a * p
            r = r - a * s
            r_ref[at, :] = r
            gamma = gamma + jnp.sum((r * r * inverse).reshape(rows_y // 8, 8, layers), axis=0)

        for d in range(n):
            c_copy(par, d).wait_send()
        for group in ranges[:0:-1]:
            wide = scatter(par, group)
            nloc_ref[...] += wide[:, :layers] + wide[:, layers:]
        wide = scatter(par, ranges[0])
        delta = jnp.zeros((8, layers), jnp.float32)
        for i in range(rows_x):
            at = slice(i * rows_y, (i + 1) * rows_y)
            z = nloc_ref[at, :] + (wide[at, :layers] + wide[at, layers:]) + b * z_ref[at, :]
            z_ref[at, :] = z
            w = w_ref[at, :] - a_w * z
            w_ref[at, :] = w
            m = w * inv_ref[at, :]
            m_ref[at, :] = m
            delta = delta + jnp.sum((m * r_ref[at, :]).reshape(rows_y // 8, 8, layers), axis=0)
        gamma = jnp.sum(gamma, axis=0, keepdims=True)
        delta = jnp.sum(delta, axis=0, keepdims=True)
        dots_ref[...] = jnp.where(
            first_half, gamma + pltpu.roll(gamma, half, 1), delta + pltpu.roll(delta, half, 1)
        )
        return gam, a

    for group in ranges:
        for d in group:
            swaps[d].wait_recv()
            for j in range(WCAP):
                slot = d * WCAP + j
                block = schur_in[slot]
                high = block.astype(jnp.bfloat16)
                schur_two[slot, 0:perf, :] = high
                schur_two[slot, perf : 2 * perf, :] = (block - high.astype(jnp.float32)).astype(jnp.bfloat16)
    for copy in swaps:
        copy.wait_send()

    ones = jnp.ones((1, layers), jnp.float32)
    gam_old, a_old = lax.fori_loop(0, ITERS, step, (ones, ones))

    par = ITERS % 2
    for d in range(n - 1, -1, -1):
        send_b[par, d, :, chunk:] = dots_ref[...]
        b_copy(par, d).start()
    for d in range(n):
        b_copy(par, d).wait_recv()
    total = start_sums(par)
    for d in range(n):
        b_copy(par, d).wait_send()
    gam, dlt = end_sums(par, total)
    b = gam / gam_old
    a = gam / (dlt - b * gam / a_old)
    for i in range(rows_x):
        at = slice(i * rows_y, (i + 1) * rows_y)
        r = r_ref[at, :]
        p = r * inv_ref[at, :] + b * p_ref[at, :]
        s = w_ref[at, :] + b * s_ref[at, :]
        x_ref[at, :] = x_ref[at, :] + a * p
        r_ref[at, :] = r - a * s


def hand_on(x_ref, r_ref, x_out, r_out):
    x_out[...] = x_ref[...]
    r_out[...] = r_ref[...]


def local(
    right_side,
    accumulation,
    trans_x,
    trans_y,
    trans_z,
    perf_cells,
    perf_live,
    well_region,
    schur_blocks,
):
    rows_x, rows_y, layers = right_side.shape
    cols = rows_x * rows_y
    wells, perf = perf_cells.shape
    n, ny = lax.axis_size("gx"), lax.axis_size("gy")
    chunk = WCAP * perf
    f32, bf16, i32 = jnp.float32, jnp.bfloat16, jnp.int32
    vmem, dma = pltpu.VMEM, pltpu.SemaphoreType.DMA
    field = vmem((cols, layers), f32)
    fields = [value.reshape(cols, layers) for value in (right_side, accumulation, trans_x, trans_y, trans_z)]
    in_vmem = pl.BlockSpec(memory_space=pltpu.VMEM)
    outs = pl.pallas_call(
        functools.partial(kernel, n, ny, rows_x, rows_y),
        out_shape=[jax.ShapeDtypeStruct((cols, layers), f32)] * 2,
        in_specs=[pl.BlockSpec(memory_space=pltpu.SMEM)]
        + [pl.BlockSpec(memory_space=pl.ANY)] * 5
        + [in_vmem] * 2
        + [pl.BlockSpec(memory_space=pl.ANY)],
        out_specs=[in_vmem] * 2,
        scratch_shapes=[field] * 5
        + [
            vmem((wells, perf, perf), f32),
            vmem((n * WCAP, perf, perf), f32),
            vmem((n * WCAP, perf, perf), f32),
            vmem((n * WCAP, 2 * perf, perf), bf16),
            vmem((cols, n * chunk), bf16),
            vmem((2 * layers, n * chunk), bf16),
            vmem((n, 1, chunk), i32),
            vmem((n, 1, chunk), i32),
            vmem((n, 1, chunk), i32),
            vmem((2, n, 1, chunk + layers), f32),
            vmem((2, n, 1, chunk + layers), f32),
            vmem((2, n, 1, chunk), f32),
            vmem((2, n, 1, chunk), f32),
            vmem((2, 1, layers), f32),
            vmem((2, ny, 1, layers), f32),
            vmem((2, 2, rows_x, layers), f32),
            vmem((2, 2, rows_y, layers), f32),
            vmem((2, 2, rows_x, layers), f32),
            vmem((rows_x, layers), f32),
            vmem((rows_y, layers), f32),
            vmem((rows_x, layers), f32),
            vmem((cols + rows_y, layers), f32),
        ]
        + [field] * 11
        + [
            vmem((1, layers), f32),
            dma,
            dma((5,)),
            dma((n,)),
            dma((n,)),
            dma((n,)),
            dma((n,)),
            dma((2,)),
            dma((2,)),
            dma((2, 4)),
            dma((2, 4)),
            dma((2, n)),
            dma((2, n)),
            dma((2, n)),
            dma((2, n)),
            dma((2, ny)),
            dma((2, ny)),
        ],
        compiler_params=pltpu.CompilerParams(
            collective_id=0, has_side_effects=True, vmem_limit_bytes=60 * 1024 * 1024
        ),
    )(well_region.reshape(1, wells), *fields, perf_cells, perf_live, schur_blocks)
    outs = pl.pallas_call(
        hand_on,
        out_shape=[jax.ShapeDtypeStruct((cols, layers), f32)] * 2,
        in_specs=[in_vmem] * 2,
        out_specs=[in_vmem] * 2,
    )(*outs)
    return tuple(value.reshape(right_side.shape) for value in outs)


def solution(mesh):
    field, rows = P("gx", "gy", None), P(("gx", "gy"), None)
    return jax.shard_map(
        local,
        mesh=mesh,
        in_specs=(field,) * 5 + (rows,) * 3 + (P(("gx", "gy"), None, None),),
        out_specs=(field, field),
        check_vma=False,
    )
```

```python
import functools

import jax
import jax.numpy as jnp
from jax import lax
from jax.experimental import pallas as pl
from jax.experimental.pallas import tpu as pltpu
from jax.sharding import PartitionSpec as P

WCAP = 2
ITERS = 6
SEND = ((7, 8), (1, 3), (3, 5), (5, 7), (0, 1))
PUSH = ((0, 1), (1, 3), (7, 8), (3, 5), (5, 7))
SCATTER = ((0, 3), (3, 5), (5, 8))
MESH = pl.DeviceIdType.MESH


def split_bf16(values):
    high = values.astype(jnp.bfloat16).astype(jnp.float32)
    return high, values - high


def kernel(
    n,
    ny,
    rows_x,
    rows_y,
    region_ref,
    rhs_hbm,
    acc_hbm,
    tx_hbm,
    ty_hbm,
    tz_hbm,
    cells_ref,
    live_ref,
    schur_hbm,
    x_ref,
    r_ref,
    rhs_ref,
    acc_ref,
    tx_ref,
    ty_ref,
    tz_ref,
    schur_vm,
    schur_out,
    schur_in,
    schur_two,
    onehot,
    vl_ref,
    lay_ref,
    req_send,
    req_recv,
    send_b,
    recv_b,
    send_c,
    recv_c,
    send_g,
    recv_g,
    ysend,
    xrecv,
    yrecv,
    yface_send,
    xface_recv,
    yface_recv,
    fx_ref,
    fy_ref,
    py_ref,
    fz_ref,
    pz_ref,
    inv_ref,
    m_ref,
    w_ref,
    z_ref,
    p_ref,
    s_ref,
    nloc_ref,
    dots_ref,
    last_send,
    last_recv,
    well_dot,
    local_sem,
    field_sem,
    schur_ss,
    schur_rs,
    req_ss,
    req_rs,
    face_ss,
    face_rs,
    halo_ss,
    halo_rs,
    b_ss,
    b_rs,
    c_ss,
    c_rs,
    g_ss,
    g_rs,
    last_ss,
    last_rs,
):
    cols, layers = rhs_ref.shape
    wells, perf = cells_ref.shape
    chunk = WCAP * perf
    shift = layers.bit_length() - 1
    assert layers == 1 << shift and n == 1 << (n.bit_length() - 1)
    me, my = lax.axis_index("gx"), lax.axis_index("gy")

    def across(d):
        peer = me
        for bit in range(n.bit_length() - 1):
            if d >> bit & 1:
                peer = peer + (1 << bit) * (1 - 2 * lax.rem(lax.div(me, 1 << bit), 2))
        return peer

    def at_peer(d):
        return {"gx": across(d)}

    def at_x(d):
        return {"gx": lax.rem(me + (d + n), n)}

    def at_y(d):
        return {"gy": lax.rem(my + (d + ny), ny)}

    def at_other():
        return {"gy": my + 1 - 2 * lax.rem(my, 2)}

    def at_cross(d):
        return {"gx": across(d), **at_other()}

    def remote(src, dst, ss, rs, where):
        return pltpu.make_async_remote_copy(
            src_ref=src, dst_ref=dst, send_sem=ss, recv_sem=rs, device_id=where, device_id_type=MESH
        )

    schur_copy = pltpu.make_async_copy(schur_hbm, schur_vm, local_sem)
    loads = [
        pltpu.make_async_copy(src, dst, field_sem.at[i])
        for i, (src, dst) in enumerate(
            (
                (ty_hbm, ty_ref),
                (tx_hbm, tx_ref),
                (tz_hbm, tz_ref),
                (acc_hbm, acc_ref),
                (rhs_hbm, rhs_ref),
            )
        )
    ]
    for copy in loads:
        copy.start()
    schur_copy.start()
    xrecv[...] = jnp.zeros_like(xrecv)
    barrier = pltpu.get_barrier_semaphore()
    others = [(d, e) for d in range(n - 1, -1, -1) for e in range(ny) if d or e]
    for d, e in others:
        pl.semaphore_signal(barrier, inc=1, device_id={"gx": across(d), **at_y(e)}, device_id_type=MESH)

    well_at = []
    for d in range(n):
        peer = across(d)
        found = [jnp.int32(0)] * WCAP
        count = jnp.int32(0)
        for w in range(wells):
            match = region_ref[0, w] == peer
            for j in range(WCAP):
                found[j] = jnp.where(jnp.logical_and(match, count == j), jnp.int32(w), found[j])
            count = count + match.astype(jnp.int32)
        well_at.append(found)
        target = req_send if d else req_recv
        for j in range(WCAP):
            used = (count > j).astype(jnp.int32)
            span = slice(j * perf, (j + 1) * perf)
            open_slot = live_ref[pl.ds(found[j], 1), :] * used
            target[d, :, span] = (cells_ref[pl.ds(found[j], 1), :] + 1) * open_slot - 1
    loads[0].wait()
    loads[1].wait()
    yface_send[...] = ty_ref[pl.ds(rows_y - 1, rows_x, stride=rows_y), :]

    pl.semaphore_wait(barrier, len(others))
    requests = [
        remote(req_send.at[d], req_recv.at[d], req_ss.at[d], req_rs.at[d], at_peer(d)) for d in range(1, n)
    ]
    face_out = [
        remote(
            tx_ref.at[pl.ds(cols - rows_y, rows_y)], xface_recv, face_ss.at[0], face_rs.at[0], at_x(1)
        ),
        remote(yface_send, yface_recv, face_ss.at[1], face_rs.at[1], at_y(1)),
    ]
    for copy in requests[::-1] + face_out:
        copy.start()

    def cut(parts):
        return [range(n * low // 8, n * high // 8) for low, high in parts]

    sends, pushes, scatters = cut(SEND), cut(PUSH), cut(SCATTER)
    swaps = [
        remote(
            schur_out.at[pl.ds(d * WCAP, WCAP)],
            schur_in.at[pl.ds(d * WCAP, WCAP)],
            schur_ss.at[d],
            schur_rs.at[d],
            at_other(),
        )
        for d in range(n)
    ]
    schur_copy.wait()
    for group in pushes:
        for d in group:
            for j in range(WCAP):
                schur_out[d * WCAP + j] = schur_vm[well_at[d][j]]
            swaps[d].start()

    last_x = me == n - 1
    last_y = my == ny - 1
    lane = lax.broadcasted_iota(jnp.int32, (rows_y, layers), 1)
    row = lax.broadcasted_iota(jnp.int32, (rows_y, layers), 0)
    zeros = jnp.zeros((rows_y, layers), jnp.float32)
    for copy in loads[2:]:
        copy.wait()
    for copy in face_out:
        copy.wait()
    fx_ref[0:rows_y, :] = jnp.where(me == 0, 0.0, xface_recv[...])
    for i in range(rows_x):
        at = slice(i * rows_y, (i + 1) * rows_y)
        after = slice((i + 1) * rows_y, (i + 2) * rows_y)
        fx = tx_ref[at, :]
        if i == rows_x - 1:
            fx = jnp.where(last_x, 0.0, fx)
        fx_ref[after, :] = fx
        fy = ty_ref[at, :]
        below = jnp.where(my == 0, 0.0, yface_recv[i : i + 1, :])
        py = jnp.where(row == 0, below, pltpu.roll(fy, 1, 0))
        fy = jnp.where(jnp.logical_and(last_y, row == rows_y - 1), 0.0, fy)
        fy_ref[at, :] = fy
        py_ref[at, :] = py
        fz = jnp.where(lane == layers - 1, 0.0, tz_ref[at, :])
        pz = pltpu.roll(fz, 1, 1)
        fz_ref[at, :] = fz
        pz_ref[at, :] = pz
        diagonal = acc_ref[at, :] + fx + fx_ref[at, :] + fy + py + fz + pz
        inverse = 1.0 / diagonal
        inv_ref[at, :] = inverse
        r = rhs_ref[at, :]
        r_ref[at, :] = r
        u = r * inverse
        m_ref[at, :] = u
        for ref in (x_ref, w_ref, z_ref, p_ref, s_ref):
            ref[at, :] = zeros
    dots_ref[...] = jnp.zeros_like(dots_ref)

    column = lax.broadcasted_iota(jnp.int32, (cols, chunk), 0)
    for d in range(n):
        if d:
            requests[d - 1].wait_recv()
        cells = req_recv[d]
        lay_ref[d] = jnp.bitwise_and(cells, layers - 1)
        onehot[:, d * chunk : (d + 1) * chunk] = (
            (column == lax.shift_right_logical(cells, shift)).astype(jnp.float32).astype(jnp.bfloat16)
        )
    for copy in requests:
        copy.wait_send()

    layer = lax.broadcasted_iota(jnp.int32, (layers, chunk), 0)
    pick_row = lax.broadcasted_iota(jnp.int32, (16, perf), 0)

    half = layers // 2
    first_half = lax.broadcasted_iota(jnp.int32, (1, layers), 1) < half

    def b_copy(par, d):
        return remote(send_b.at[par, d], recv_b.at[par, d], b_ss.at[par, d], b_rs.at[par, d], at_cross(d))

    def c_copy(par, d):
        return remote(send_c.at[par, d], recv_c.at[par, d], c_ss.at[par, d], c_rs.at[par, d], at_cross(d))

    def g_copy(par, d, slot):
        return remote(send_g.at[par], recv_g.at[par, slot], g_ss.at[par, d], g_rs.at[par, slot], at_y(d))

    def halo_copies(par):
        return [
            remote(
                m_ref.at[pl.ds(cols - rows_y, rows_y)],
                xrecv.at[par, 0],
                halo_ss.at[par, 0],
                halo_rs.at[par, 0],
                at_x(1),
            ),
            remote(
                m_ref.at[pl.ds(0, rows_y)], xrecv.at[par, 1], halo_ss.at[par, 1], halo_rs.at[par, 1], at_x(-1)
            ),
            remote(ysend.at[par, 0], yrecv.at[par, 0], halo_ss.at[par, 2], halo_rs.at[par, 2], at_y(1)),
            remote(ysend.at[par, 1], yrecv.at[par, 1], halo_ss.at[par, 3], halo_rs.at[par, 3], at_y(-1)),
        ]

    def start_sums(par):
        total = recv_b[par, 0, :, chunk:]
        for d in range(1, n):
            total = total + recv_b[par, d, :, chunk:]
        send_g[par] = total
        for d in range(1, ny):
            g_copy(par, d, ny - d).start()
        return total

    def end_sums(par, total):
        for d in range(1, ny):
            g_copy(par, d, d).wait_recv()
            total = total + recv_g[par, d]
        for d in range(1, ny):
            g_copy(par, d, d).wait_send()
        gam = jnp.sum(jnp.where(first_half, total, 0.0), axis=1, keepdims=True)
        dlt = jnp.sum(jnp.where(first_half, 0.0, total), axis=1, keepdims=True)
        return jnp.broadcast_to(gam, (1, layers)), jnp.broadcast_to(dlt, (1, layers))

    def start_halos(par):
        ysend[par, 0] = m_ref[pl.ds(rows_y - 1, rows_x, stride=rows_y), :]
        ysend[par, 1] = m_ref[pl.ds(0, rows_x, stride=rows_y), :]
        halos = halo_copies(par)
        pl.when(me < n - 1)(halos[0].start)
        pl.when(me > 0)(halos[1].start)
        for copy in halos[2:]:
            copy.start()

    def send_field(par):
        high, low = split_bf16(m_ref[...].T)
        lhs = jnp.concatenate([high, low], 0).astype(jnp.bfloat16)
        dots = dots_ref[...]
        for group in sends:
            for d in group:
                part = jnp.dot(
                    lhs, onehot[:, d * chunk : (d + 1) * chunk], preferred_element_type=jnp.float32
                )
                part = part[:layers] + part[layers:]
                picked = jnp.sum(jnp.where(layer == lay_ref[d], part, 0.0), axis=0, keepdims=True)
                send_b[par, d, :, :chunk] = picked
                send_b[par, d, :, chunk:] = dots
            for d in group:
                b_copy(par, d).start()
            if group is sends[0]:
                start_halos(par)

    def stencil(par):
        halos = halo_copies(par)
        x_up, x_down = halos[:2]

        @pl.when(me < n - 1)
        def _():
            x_up.wait_send()
            x_down.wait_recv()

        @pl.when(me > 0)
        def _():
            x_up.wait_recv()
            x_down.wait_send()

        for copy in halos[2:]:
            copy.wait()
        for i in range(rows_x):
            at = slice(i * rows_y, (i + 1) * rows_y)
            after = slice((i + 1) * rows_y, (i + 2) * rows_y)
            m = m_ref[at, :]
            below = m_ref[(i - 1) * rows_y : i * rows_y, :] if i else xrecv[par, 0]
            above = m_ref[after, :] if i < rows_x - 1 else xrecv[par, 1]
            y_prev = jnp.where(row == 0, yrecv[par, 0, i : i + 1, :], pltpu.roll(m, 1, 0))
            y_next = jnp.where(row == rows_y - 1, yrecv[par, 1, i : i + 1, :], pltpu.roll(m, rows_y - 1, 0))
            nloc_ref[at, :] = (
                acc_ref[at, :] * m
                + fx_ref[after, :] * (m - above)
                + fx_ref[at, :] * (m - below)
                + fy_ref[at, :] * (m - y_next)
                + py_ref[at, :] * (m - y_prev)
                + fz_ref[at, :] * (m - pltpu.roll(m, layers - 1, 1))
                + pz_ref[at, :] * (m - pltpu.roll(m, 1, 1))
            )

    def push(par, keep=False):
        for group in pushes:
            for d in group:
                b_copy(par, d).wait_recv()
            for d in group:
                for j in range(WCAP):
                    span = slice(j * perf, (j + 1) * perf)
                    high, low = split_bf16(recv_b[par, d, :, span])
                    left = jnp.where(pick_row == 0, high, jnp.where(pick_row == 1, low, 0.0)).astype(
                        jnp.bfloat16
                    )
                    pushed = jnp.dot(
                        jnp.concatenate([left, left], 1),
                        schur_two[d * WCAP + j],
                        preferred_element_type=jnp.float32,
                    )
                    pushed = jnp.sum(pushed, axis=0, keepdims=True)
                    send_c[par, d, :, span] = pushed
                    if keep:
                        part = recv_b[par, d, :, span] * pushed
                        for low_lane in range(0, perf, layers):
                            well_dot[...] += part[:, low_lane : low_lane + layers]
            for d in group:
                c_copy(par, d).start()

    def scatter(par, group):
        for d in group:
            c_copy(par, d).wait_recv()
        for d in group:
            high, low = split_bf16(recv_c[par, d])
            here = layer == lay_ref[d]
            span = slice(d * chunk, (d + 1) * chunk)
            vl_ref[0:layers, span] = jnp.where(here, high, 0.0).astype(jnp.bfloat16)
            vl_ref[layers : 2 * layers, span] = jnp.where(here, low, 0.0).astype(jnp.bfloat16)
        span = slice(group[0] * chunk, (group[-1] + 1) * chunk)
        return lax.dot_general(
            onehot[:, span],
            vl_ref[:, span],
            (((1,), (1,)), ((), ())),
            preferred_element_type=jnp.float32,
        )

    def advance(a, b):
        gamma = jnp.zeros((8, layers), jnp.float32)
        for i in range(rows_x):
            at = slice(i * rows_y, (i + 1) * rows_y)
            inverse = inv_ref[at, :]
            r = r_ref[at, :]
            p = r * inverse + b * p_ref[at, :]
            s = w_ref[at, :] + b * s_ref[at, :]
            p_ref[at, :] = p
            s_ref[at, :] = s
            x_ref[at, :] = x_ref[at, :] + a * p
            r = r - a * s
            r_ref[at, :] = r
            gamma = gamma + jnp.sum((r * r * inverse).reshape(rows_y // 8, 8, layers), axis=0)
        return gamma

    def tiles(values):
        return jnp.sum(values.reshape(rows_y // 8, 8, layers), axis=0)

    def last_copy(d, e):
        slot = d * ny + (ny - e) % ny
        return remote(
            last_send, last_recv.at[slot], last_ss, last_rs, {"gx": across(d), **at_y(e)}
        )

    def step(k, carried):
        gam_old, a_old = carried
        par = lax.rem(k, 2)
        send_field(par)
        push(par)
        total = start_sums(par)
        stencil(par)
        for group in scatters[:-1]:
            wide = scatter(par, group)
            nloc_ref[...] += wide[:, :layers] + wide[:, layers:]
        for d in range(n):
            b_copy(par, d).wait_send()
            c_copy(par, d).wait_send()
        gam, dlt = end_sums(par, total)
        b = jnp.where(k <= 1, 0.0, gam / gam_old)
        a = jnp.where(k == 0, 0.0, jnp.where(k == 1, gam / dlt, gam / (dlt - b * gam / a_old)))
        a_w = jnp.where(k == 0, -1.0, a)
        gamma = advance(a, b)
        wide = scatter(par, scatters[-1])
        delta = jnp.zeros((8, layers), jnp.float32)
        for i in range(rows_x):
            at = slice(i * rows_y, (i + 1) * rows_y)
            z = nloc_ref[at, :] + (wide[at, :layers] + wide[at, layers:]) + b * z_ref[at, :]
            z_ref[at, :] = z
            w = w_ref[at, :] - a_w * z
            w_ref[at, :] = w
            m = w * inv_ref[at, :]
            m_ref[at, :] = m
            delta = delta + jnp.sum((m * r_ref[at, :]).reshape(rows_y // 8, 8, layers), axis=0)
        gamma = jnp.sum(gamma, axis=0, keepdims=True)
        delta = jnp.sum(delta, axis=0, keepdims=True)
        dots_ref[...] = jnp.where(
            first_half, gamma + pltpu.roll(gamma, half, 1), delta + pltpu.roll(delta, half, 1)
        )
        return gam, a

    for group in pushes:
        for d in group:
            swaps[d].wait_recv()
            for j in range(WCAP):
                slot = d * WCAP + j
                block = schur_in[slot]
                high = block.astype(jnp.bfloat16)
                schur_two[slot, 0:perf, :] = high
                schur_two[slot, perf : 2 * perf, :] = (block - high.astype(jnp.float32)).astype(jnp.bfloat16)
    for copy in swaps:
        copy.wait_send()

    ones = jnp.ones((1, layers), jnp.float32)
    gam_old, a_old = lax.fori_loop(0, ITERS - 1, step, (ones, ones))

    par = (ITERS - 1) % 2
    send_field(par)
    zero = jnp.zeros((8, layers), jnp.float32)
    sums = [zero] * 6
    for i in range(rows_x):
        at = slice(i * rows_y, (i + 1) * rows_y)
        inverse, w, s, z, m = inv_ref[at, :], w_ref[at, :], s_ref[at, :], z_ref[at, :], m_ref[at, :]
        q = s * inverse
        terms = (w * m, q * r_ref[at, :], s * m, s * q, z * m, z * q)
        sums = [total + tiles(term) for total, term in zip(sums, terms)]
    well_dot[...] = jnp.zeros_like(well_dot)
    push(par, keep=True)
    total = start_sums(par)
    stencil(par)
    image_dot = zero
    for i in range(rows_x):
        at = slice(i * rows_y, (i + 1) * rows_y)
        image_dot = image_dot + tiles(m_ref[at, :] * nloc_ref[at, :])
    rows = [jnp.sum(value, axis=0, keepdims=True) for value in sums + [image_dot]]
    rows[-1] = rows[-1] + well_dot[...]
    values = len(rows) + 1
    width = layers // values
    lane_row = lax.broadcasted_iota(jnp.int32, (1, layers), 1)
    packed = jnp.zeros((1, layers), jnp.float32)
    for index, value in enumerate(rows):
        fold = half
        while fold >= width:
            value = value + pltpu.roll(value, fold, 1)
            fold //= 2
        packed = jnp.where(lane_row // width == index, value, packed)
    last_send[...] = packed
    for d, e in others:
        last_copy(d, e).start()
    for group in scatters[:-1]:
        wide = scatter(par, group)
        nloc_ref[...] += wide[:, :layers] + wide[:, layers:]
    for d in range(n):
        b_copy(par, d).wait_send()
        c_copy(par, d).wait_send()
    gam, dlt = end_sums(par, total)
    b = gam / gam_old
    a = gam / (dlt - b * gam / a_old)
    advance(a, b)
    wide = scatter(par, scatters[-1])
    arrived = last_recv.at[pl.ds(1, len(others))]
    pltpu.make_async_copy(arrived, arrived, last_rs).wait()
    pltpu.make_async_copy(arrived, arrived, last_ss).wait()
    packed = last_send[...]
    for slot in range(1, len(others) + 1):
        packed = packed + last_recv[slot]

    def value_of(index):
        value = jnp.sum(jnp.where(lane_row // width == index, packed, 0.0), axis=1, keepdims=True)
        return jnp.broadcast_to(value, (1, layers))

    wm, su, sm, sq, zm, zq, am = [value_of(index) for index in range(len(rows))]
    gam_new = gam - 2.0 * a * (dlt + b * su) + a * a * (wm + 2.0 * b * sm + b * b * sq)
    dlt_new = dlt - 2.0 * a * (wm + b * sm) + a * a * (am + 2.0 * b * zm + b * b * zq)
    b_new = gam_new / gam
    a_new = gam_new / (dlt_new - b_new * gam_new / a)
    for i in range(rows_x):
        at = slice(i * rows_y, (i + 1) * rows_y)
        z = nloc_ref[at, :] + (wide[at, :layers] + wide[at, layers:]) + b * z_ref[at, :]
        w = w_ref[at, :] - a * z
        r = r_ref[at, :]
        p = r * inv_ref[at, :] + b_new * p_ref[at, :]
        s = w + b_new * s_ref[at, :]
        x_ref[at, :] = x_ref[at, :] + a_new * p
        r_ref[at, :] = r - a_new * s


def hand_on(x_ref, r_ref, x_out, r_out):
    x_out[...] = x_ref[...]
    r_out[...] = r_ref[...]


def local(
    right_side,
    accumulation,
    trans_x,
    trans_y,
    trans_z,
    perf_cells,
    perf_live,
    well_region,
    schur_blocks,
):
    rows_x, rows_y, layers = right_side.shape
    cols = rows_x * rows_y
    wells, perf = perf_cells.shape
    n, ny = lax.axis_size("gx"), lax.axis_size("gy")
    chunk = WCAP * perf
    f32, bf16, i32 = jnp.float32, jnp.bfloat16, jnp.int32
    vmem, dma = pltpu.VMEM, pltpu.SemaphoreType.DMA
    field = vmem((cols, layers), f32)
    fields = [value.reshape(cols, layers) for value in (right_side, accumulation, trans_x, trans_y, trans_z)]
    in_vmem = pl.BlockSpec(memory_space=pltpu.VMEM)
    outs = pl.pallas_call(
        functools.partial(kernel, n, ny, rows_x, rows_y),
        out_shape=[jax.ShapeDtypeStruct((cols, layers), f32)] * 2,
        in_specs=[pl.BlockSpec(memory_space=pltpu.SMEM)]
        + [pl.BlockSpec(memory_space=pl.ANY)] * 5
        + [in_vmem] * 2
        + [pl.BlockSpec(memory_space=pl.ANY)],
        out_specs=[in_vmem] * 2,
        scratch_shapes=[field] * 5
        + [
            vmem((wells, perf, perf), f32),
            vmem((n * WCAP, perf, perf), f32),
            vmem((n * WCAP, perf, perf), f32),
            vmem((n * WCAP, 2 * perf, perf), bf16),
            vmem((cols, n * chunk), bf16),
            vmem((2 * layers, n * chunk), bf16),
            vmem((n, 1, chunk), i32),
            vmem((n, 1, chunk), i32),
            vmem((n, 1, chunk), i32),
            vmem((2, n, 1, chunk + layers), f32),
            vmem((2, n, 1, chunk + layers), f32),
            vmem((2, n, 1, chunk), f32),
            vmem((2, n, 1, chunk), f32),
            vmem((2, 1, layers), f32),
            vmem((2, ny, 1, layers), f32),
            vmem((2, 2, rows_x, layers), f32),
            vmem((2, 2, rows_y, layers), f32),
            vmem((2, 2, rows_x, layers), f32),
            vmem((rows_x, layers), f32),
            vmem((rows_y, layers), f32),
            vmem((rows_x, layers), f32),
            vmem((cols + rows_y, layers), f32),
        ]
        + [field] * 11
        + [
            vmem((1, layers), f32),
            vmem((1, layers), f32),
            vmem((n * ny, 1, layers), f32),
            vmem((1, layers), f32),
            dma,
            dma((5,)),
            dma((n,)),
            dma((n,)),
            dma((n,)),
            dma((n,)),
            dma((2,)),
            dma((2,)),
            dma((2, 4)),
            dma((2, 4)),
            dma((2, n)),
            dma((2, n)),
            dma((2, n)),
            dma((2, n)),
            dma((2, ny)),
            dma((2, ny)),
            dma,
            dma,
        ],
        compiler_params=pltpu.CompilerParams(
            collective_id=0, has_side_effects=True, vmem_limit_bytes=60 * 1024 * 1024
        ),
    )(well_region.reshape(1, wells), *fields, perf_cells, perf_live, schur_blocks)
    outs = pl.pallas_call(
        hand_on,
        out_shape=[jax.ShapeDtypeStruct((cols, layers), f32)] * 2,
        in_specs=[in_vmem] * 2,
        out_specs=[in_vmem] * 2,
    )(*outs)
    return tuple(value.reshape(right_side.shape) for value in outs)


def solution(mesh):
    field, rows = P("gx", "gy", None), P(("gx", "gy"), None)
    return jax.shard_map(
        local,
        mesh=mesh,
        in_specs=(field,) * 5 + (rows,) * 3 + (P(("gx", "gy"), None, None),),
        out_specs=(field, field),
        check_vma=False,
    )
```

```python
import functools

import jax
import jax.numpy as jnp
from jax import lax
from jax.experimental import pallas as pl
from jax.experimental.pallas import tpu as pltpu
from jax.sharding import PartitionSpec as P

WCAP = 2
ITERS = 6
SEND = ((7, 8), (1, 3), (3, 5), (5, 7), (0, 1))
PUSH = ((0, 1), (1, 3), (7, 8), (3, 5), (5, 7))
SCATTER = ((0, 3), (3, 5), (5, 8))
MESH = pl.DeviceIdType.MESH


def split_bf16(values):
    high = values.astype(jnp.bfloat16).astype(jnp.float32)
    return high, values - high


def kernel(
    n,
    ny,
    rows_x,
    rows_y,
    region_hbm,
    rhs_hbm,
    acc_hbm,
    tx_hbm,
    ty_hbm,
    tz_hbm,
    cells_hbm,
    live_hbm,
    schur_hbm,
    x_ref,
    r_ref,
    region_ref,
    cells_ref,
    live_ref,
    rhs_ref,
    acc_ref,
    tx_ref,
    ty_ref,
    tz_ref,
    schur_vm,
    schur_out,
    schur_in,
    schur_two,
    onehot,
    vl_ref,
    lay_ref,
    req_send,
    req_recv,
    send_b,
    recv_b,
    send_c,
    recv_c,
    send_g,
    recv_g,
    ysend,
    xrecv,
    yrecv,
    yface_send,
    xface_recv,
    yface_recv,
    fx_ref,
    fy_ref,
    py_ref,
    fz_ref,
    pz_ref,
    inv_ref,
    m_ref,
    w_ref,
    z_ref,
    p_ref,
    s_ref,
    nloc_ref,
    dots_ref,
    last_send,
    last_recv,
    well_dot,
    local_sem,
    field_sem,
    small_sem,
    schur_ss,
    schur_rs,
    req_ss,
    req_rs,
    face_ss,
    face_rs,
    halo_ss,
    halo_rs,
    b_ss,
    b_rs,
    c_ss,
    c_rs,
    g_ss,
    g_rs,
    last_ss,
    last_rs,
):
    cols, layers = rhs_ref.shape
    wells, perf = cells_ref.shape
    chunk = WCAP * perf
    shift = layers.bit_length() - 1
    assert layers == 1 << shift and n == 1 << (n.bit_length() - 1)
    me, my = lax.axis_index("gx"), lax.axis_index("gy")

    def across(d):
        peer = me
        for bit in range(n.bit_length() - 1):
            if d >> bit & 1:
                peer = peer + (1 << bit) * (1 - 2 * lax.rem(lax.div(me, 1 << bit), 2))
        return peer

    def at_peer(d):
        return {"gx": across(d)}

    def at_x(d):
        return {"gx": lax.rem(me + (d + n), n)}

    def at_y(d):
        return {"gy": lax.rem(my + (d + ny), ny)}

    def at_other():
        return {"gy": my + 1 - 2 * lax.rem(my, 2)}

    def at_cross(d):
        return {"gx": across(d), **at_other()}

    def remote(src, dst, ss, rs, where):
        return pltpu.make_async_remote_copy(
            src_ref=src, dst_ref=dst, send_sem=ss, recv_sem=rs, device_id=where, device_id_type=MESH
        )

    schur_copy = pltpu.make_async_copy(schur_hbm, schur_vm, local_sem)
    loads = [
        pltpu.make_async_copy(src, dst, field_sem.at[i])
        for i, (src, dst) in enumerate(
            (
                (ty_hbm, ty_ref),
                (tx_hbm, tx_ref),
                (tz_hbm, tz_ref),
                (acc_hbm, acc_ref),
                (rhs_hbm, rhs_ref),
            )
        )
    ]
    small = [
        pltpu.make_async_copy(src, dst, small_sem.at[i])
        for i, (src, dst) in enumerate(
            ((region_hbm, region_ref), (cells_hbm, cells_ref), (live_hbm, live_ref))
        )
    ]
    for copy in small:
        copy.start()
    barrier = pltpu.get_barrier_semaphore()
    others = [(d, e) for d in range(n - 1, -1, -1) for e in range(ny) if d or e]
    for d, e in others:
        pl.semaphore_signal(barrier, inc=1, device_id={"gx": across(d), **at_y(e)}, device_id_type=MESH)

    for copy in loads:
        copy.start()
    schur_copy.start()
    xrecv[...] = jnp.zeros_like(xrecv)
    for copy in small:
        copy.wait()

    well_at = []
    for d in range(n):
        peer = across(d)
        found = [jnp.int32(0)] * WCAP
        count = jnp.int32(0)
        for w in range(wells):
            match = region_ref[0, w] == peer
            for j in range(WCAP):
                found[j] = jnp.where(jnp.logical_and(match, count == j), jnp.int32(w), found[j])
            count = count + match.astype(jnp.int32)
        well_at.append(found)
        target = req_send if d else req_recv
        for j in range(WCAP):
            used = (count > j).astype(jnp.int32)
            span = slice(j * perf, (j + 1) * perf)
            open_slot = live_ref[pl.ds(found[j], 1), :] * used
            target[d, :, span] = (cells_ref[pl.ds(found[j], 1), :] + 1) * open_slot - 1
    loads[0].wait()
    loads[1].wait()
    yface_send[...] = ty_ref[pl.ds(rows_y - 1, rows_x, stride=rows_y), :]

    pl.semaphore_wait(barrier, len(others))
    requests = [
        remote(req_send.at[d], req_recv.at[d], req_ss.at[d], req_rs.at[d], at_peer(d)) for d in range(1, n)
    ]
    face_out = [
        remote(
            tx_ref.at[pl.ds(cols - rows_y, rows_y)], xface_recv, face_ss.at[0], face_rs.at[0], at_x(1)
        ),
        remote(yface_send, yface_recv, face_ss.at[1], face_rs.at[1], at_y(1)),
    ]
    for copy in requests[::-1] + face_out:
        copy.start()

    def cut(parts):
        return [range(n * low // 8, n * high // 8) for low, high in parts]

    sends, pushes, scatters = cut(SEND), cut(PUSH), cut(SCATTER)
    swaps = [
        remote(
            schur_out.at[pl.ds(d * WCAP, WCAP)],
            schur_in.at[pl.ds(d * WCAP, WCAP)],
            schur_ss.at[d],
            schur_rs.at[d],
            at_other(),
        )
        for d in range(n)
    ]
    schur_copy.wait()
    for group in pushes:
        for d in group:
            for j in range(WCAP):
                schur_out[d * WCAP + j] = schur_vm[well_at[d][j]]
            swaps[d].start()

    last_x = me == n - 1
    last_y = my == ny - 1
    lane = lax.broadcasted_iota(jnp.int32, (rows_y, layers), 1)
    row = lax.broadcasted_iota(jnp.int32, (rows_y, layers), 0)
    zeros = jnp.zeros((rows_y, layers), jnp.float32)
    column = lax.broadcasted_iota(jnp.int32, (cols, chunk), 0)

    def mark_slots(group):
        for d in group:
            if d:
                requests[d - 1].wait_recv()
            cells = req_recv[d]
            lay_ref[d] = jnp.bitwise_and(cells, layers - 1)
            onehot[:, d * chunk : (d + 1) * chunk] = (
                (column == lax.shift_right_logical(cells, shift)).astype(jnp.float32).astype(jnp.bfloat16)
            )

    mark_slots(range(n * 5 // 8))
    for copy in loads[2:]:
        copy.wait()
    for copy in face_out:
        copy.wait()
    fx_ref[0:rows_y, :] = jnp.where(me == 0, 0.0, xface_recv[...])
    for i in range(rows_x):
        at = slice(i * rows_y, (i + 1) * rows_y)
        after = slice((i + 1) * rows_y, (i + 2) * rows_y)
        fx = tx_ref[at, :]
        if i == rows_x - 1:
            fx = jnp.where(last_x, 0.0, fx)
        fx_ref[after, :] = fx
        fy = ty_ref[at, :]
        below = jnp.where(my == 0, 0.0, yface_recv[i : i + 1, :])
        py = jnp.where(row == 0, below, pltpu.roll(fy, 1, 0))
        fy = jnp.where(jnp.logical_and(last_y, row == rows_y - 1), 0.0, fy)
        fy_ref[at, :] = fy
        py_ref[at, :] = py
        fz = jnp.where(lane == layers - 1, 0.0, tz_ref[at, :])
        pz = pltpu.roll(fz, 1, 1)
        fz_ref[at, :] = fz
        pz_ref[at, :] = pz
        diagonal = acc_ref[at, :] + fx + fx_ref[at, :] + fy + py + fz + pz
        inverse = 1.0 / diagonal
        inv_ref[at, :] = inverse
        r = rhs_ref[at, :]
        r_ref[at, :] = r
        u = r * inverse
        m_ref[at, :] = u
        for ref in (x_ref, w_ref, z_ref, p_ref, s_ref):
            ref[at, :] = zeros
    dots_ref[...] = jnp.zeros_like(dots_ref)

    mark_slots(range(n * 5 // 8, n))
    for copy in requests:
        copy.wait_send()

    layer = lax.broadcasted_iota(jnp.int32, (layers, chunk), 0)
    pick_row = lax.broadcasted_iota(jnp.int32, (16, perf), 0)

    half = layers // 2
    first_half = lax.broadcasted_iota(jnp.int32, (1, layers), 1) < half

    def b_copy(par, d):
        return remote(send_b.at[par, d], recv_b.at[par, d], b_ss.at[par, d], b_rs.at[par, d], at_cross(d))

    def c_copy(par, d):
        return remote(send_c.at[par, d], recv_c.at[par, d], c_ss.at[par, d], c_rs.at[par, d], at_cross(d))

    def g_copy(par, d, slot):
        return remote(send_g.at[par], recv_g.at[par, slot], g_ss.at[par, d], g_rs.at[par, slot], at_y(d))

    def halo_copies(par):
        return [
            remote(
                m_ref.at[pl.ds(cols - rows_y, rows_y)],
                xrecv.at[par, 0],
                halo_ss.at[par, 0],
                halo_rs.at[par, 0],
                at_x(1),
            ),
            remote(
                m_ref.at[pl.ds(0, rows_y)], xrecv.at[par, 1], halo_ss.at[par, 1], halo_rs.at[par, 1], at_x(-1)
            ),
            remote(ysend.at[par, 0], yrecv.at[par, 0], halo_ss.at[par, 2], halo_rs.at[par, 2], at_y(1)),
            remote(ysend.at[par, 1], yrecv.at[par, 1], halo_ss.at[par, 3], halo_rs.at[par, 3], at_y(-1)),
        ]

    def start_sums(par):
        total = recv_b[par, 0, :, chunk:]
        for d in range(1, n):
            total = total + recv_b[par, d, :, chunk:]
        send_g[par] = total
        for d in range(1, ny):
            g_copy(par, d, ny - d).start()
        return total

    def end_sums(par, total):
        for d in range(1, ny):
            g_copy(par, d, d).wait_recv()
            total = total + recv_g[par, d]
        for d in range(1, ny):
            g_copy(par, d, d).wait_send()
        gam = jnp.sum(jnp.where(first_half, total, 0.0), axis=1, keepdims=True)
        dlt = jnp.sum(jnp.where(first_half, 0.0, total), axis=1, keepdims=True)
        return jnp.broadcast_to(gam, (1, layers)), jnp.broadcast_to(dlt, (1, layers))

    def start_halos(par):
        ysend[par, 0] = m_ref[pl.ds(rows_y - 1, rows_x, stride=rows_y), :]
        ysend[par, 1] = m_ref[pl.ds(0, rows_x, stride=rows_y), :]
        halos = halo_copies(par)
        pl.when(me < n - 1)(halos[0].start)
        pl.when(me > 0)(halos[1].start)
        for copy in halos[2:]:
            copy.start()

    def send_field(par):
        high, low = split_bf16(m_ref[...].T)
        lhs = jnp.concatenate([high, low], 0).astype(jnp.bfloat16)
        dots = dots_ref[...]
        for group in sends:
            for d in group:
                part = jnp.dot(
                    lhs, onehot[:, d * chunk : (d + 1) * chunk], preferred_element_type=jnp.float32
                )
                part = part[:layers] + part[layers:]
                picked = jnp.sum(jnp.where(layer == lay_ref[d], part, 0.0), axis=0, keepdims=True)
                send_b[par, d, :, :chunk] = picked
                send_b[par, d, :, chunk:] = dots
            for d in group:
                b_copy(par, d).start()
            if group is sends[0]:
                start_halos(par)

    def stencil(par):
        halos = halo_copies(par)
        x_up, x_down = halos[:2]

        @pl.when(me < n - 1)
        def _():
            x_up.wait_send()
            x_down.wait_recv()

        @pl.when(me > 0)
        def _():
            x_up.wait_recv()
            x_down.wait_send()

        for copy in halos[2:]:
            copy.wait()
        for i in range(rows_x):
            at = slice(i * rows_y, (i + 1) * rows_y)
            after = slice((i + 1) * rows_y, (i + 2) * rows_y)
            m = m_ref[at, :]
            below = m_ref[(i - 1) * rows_y : i * rows_y, :] if i else xrecv[par, 0]
            above = m_ref[after, :] if i < rows_x - 1 else xrecv[par, 1]
            y_prev = jnp.where(row == 0, yrecv[par, 0, i : i + 1, :], pltpu.roll(m, 1, 0))
            y_next = jnp.where(row == rows_y - 1, yrecv[par, 1, i : i + 1, :], pltpu.roll(m, rows_y - 1, 0))
            nloc_ref[at, :] = (
                acc_ref[at, :] * m
                + fx_ref[after, :] * (m - above)
                + fx_ref[at, :] * (m - below)
                + fy_ref[at, :] * (m - y_next)
                + py_ref[at, :] * (m - y_prev)
                + fz_ref[at, :] * (m - pltpu.roll(m, layers - 1, 1))
                + pz_ref[at, :] * (m - pltpu.roll(m, 1, 1))
            )

    def push(par, keep=False):
        for group in pushes:
            for d in group:
                b_copy(par, d).wait_recv()
            for d in group:
                for j in range(WCAP):
                    span = slice(j * perf, (j + 1) * perf)
                    high, low = split_bf16(recv_b[par, d, :, span])
                    left = jnp.where(pick_row == 0, high, jnp.where(pick_row == 1, low, 0.0)).astype(
                        jnp.bfloat16
                    )
                    pushed = jnp.dot(
                        jnp.concatenate([left, left], 1),
                        schur_two[d * WCAP + j],
                        preferred_element_type=jnp.float32,
                    )
                    pushed = jnp.sum(pushed, axis=0, keepdims=True)
                    send_c[par, d, :, span] = pushed
                    if keep:
                        part = recv_b[par, d, :, span] * pushed
                        for low_lane in range(0, perf, layers):
                            well_dot[...] += part[:, low_lane : low_lane + layers]
            for d in group:
                c_copy(par, d).start()

    def scatter(par, group):
        for d in group:
            c_copy(par, d).wait_recv()
        for d in group:
            high, low = split_bf16(recv_c[par, d])
            here = layer == lay_ref[d]
            span = slice(d * chunk, (d + 1) * chunk)
            vl_ref[0:layers, span] = jnp.where(here, high, 0.0).astype(jnp.bfloat16)
            vl_ref[layers : 2 * layers, span] = jnp.where(here, low, 0.0).astype(jnp.bfloat16)
        span = slice(group[0] * chunk, (group[-1] + 1) * chunk)
        return lax.dot_general(
            onehot[:, span],
            vl_ref[:, span],
            (((1,), (1,)), ((), ())),
            preferred_element_type=jnp.float32,
        )

    def advance(a, b):
        gamma = jnp.zeros((8, layers), jnp.float32)
        for i in range(rows_x):
            at = slice(i * rows_y, (i + 1) * rows_y)
            inverse = inv_ref[at, :]
            r = r_ref[at, :]
            p = r * inverse + b * p_ref[at, :]
            s = w_ref[at, :] + b * s_ref[at, :]
            p_ref[at, :] = p
            s_ref[at, :] = s
            x_ref[at, :] = x_ref[at, :] + a * p
            r = r - a * s
            r_ref[at, :] = r
            gamma = gamma + jnp.sum((r * r * inverse).reshape(rows_y // 8, 8, layers), axis=0)
        return gamma

    def tiles(values):
        return jnp.sum(values.reshape(rows_y // 8, 8, layers), axis=0)

    def last_copy(d, e):
        slot = d * ny + (ny - e) % ny
        return remote(
            last_send, last_recv.at[slot], last_ss, last_rs, {"gx": across(d), **at_y(e)}
        )

    def step(k, carried):
        gam_old, a_old = carried
        par = lax.rem(k, 2)
        push(par)
        total = start_sums(par)
        stencil(par)
        for group in scatters[:-1]:
            wide = scatter(par, group)
            nloc_ref[...] += wide[:, :layers] + wide[:, layers:]
        for d in range(n):
            b_copy(par, d).wait_send()
            c_copy(par, d).wait_send()
        gam, dlt = end_sums(par, total)
        b = jnp.where(k <= 1, 0.0, gam / gam_old)
        a = jnp.where(k == 0, 0.0, jnp.where(k == 1, gam / dlt, gam / (dlt - b * gam / a_old)))
        a_w = jnp.where(k == 0, -1.0, a)
        gamma = advance(a, b)
        wide = scatter(par, scatters[-1])
        delta = jnp.zeros((8, layers), jnp.float32)
        for i in range(rows_x):
            at = slice(i * rows_y, (i + 1) * rows_y)
            z = nloc_ref[at, :] + (wide[at, :layers] + wide[at, layers:]) + b * z_ref[at, :]
            z_ref[at, :] = z
            w = w_ref[at, :] - a_w * z
            w_ref[at, :] = w
            m = w * inv_ref[at, :]
            m_ref[at, :] = m
            delta = delta + jnp.sum((m * r_ref[at, :]).reshape(rows_y // 8, 8, layers), axis=0)
        gamma = jnp.sum(gamma, axis=0, keepdims=True)
        delta = jnp.sum(delta, axis=0, keepdims=True)
        dots_ref[...] = jnp.where(
            first_half, gamma + pltpu.roll(gamma, half, 1), delta + pltpu.roll(delta, half, 1)
        )
        send_field(lax.rem(k + 1, 2))
        return gam, a

    send_field(0)
    for group in pushes:
        for d in group:
            swaps[d].wait_recv()
            for j in range(WCAP):
                slot = d * WCAP + j
                block = schur_in[slot]
                high = block.astype(jnp.bfloat16)
                schur_two[slot, 0:perf, :] = high
                schur_two[slot, perf : 2 * perf, :] = (block - high.astype(jnp.float32)).astype(jnp.bfloat16)
    for copy in swaps:
        copy.wait_send()

    ones = jnp.ones((1, layers), jnp.float32)
    gam_old, a_old = lax.fori_loop(0, ITERS - 1, step, (ones, ones))

    par = (ITERS - 1) % 2
    zero = jnp.zeros((8, layers), jnp.float32)
    sums = [zero] * 6
    for i in range(rows_x):
        at = slice(i * rows_y, (i + 1) * rows_y)
        inverse, w, s, z, m = inv_ref[at, :], w_ref[at, :], s_ref[at, :], z_ref[at, :], m_ref[at, :]
        q = s * inverse
        terms = (w * m, q * r_ref[at, :], s * m, s * q, z * m, z * q)
        sums = [total + tiles(term) for total, term in zip(sums, terms)]
    well_dot[...] = jnp.zeros_like(well_dot)
    push(par, keep=True)
    total = start_sums(par)
    stencil(par)
    image_dot = zero
    for i in range(rows_x):
        at = slice(i * rows_y, (i + 1) * rows_y)
        image_dot = image_dot + tiles(m_ref[at, :] * nloc_ref[at, :])
    rows = [jnp.sum(value, axis=0, keepdims=True) for value in sums + [image_dot]]
    rows[-1] = rows[-1] + well_dot[...]
    values = len(rows) + 1
    width = layers // values
    lane_row = lax.broadcasted_iota(jnp.int32, (1, layers), 1)
    packed = jnp.zeros((1, layers), jnp.float32)
    for index, value in enumerate(rows):
        fold = half
        while fold >= width:
            value = value + pltpu.roll(value, fold, 1)
            fold //= 2
        packed = jnp.where(lane_row // width == index, value, packed)
    last_send[...] = packed
    for d, e in others:
        last_copy(d, e).start()
    for group in scatters[:-1]:
        wide = scatter(par, group)
        nloc_ref[...] += wide[:, :layers] + wide[:, layers:]
    for d in range(n):
        b_copy(par, d).wait_send()
        c_copy(par, d).wait_send()
    gam, dlt = end_sums(par, total)
    b = gam / gam_old
    a = gam / (dlt - b * gam / a_old)
    advance(a, b)
    wide = scatter(par, scatters[-1])
    arrived = last_recv.at[pl.ds(1, len(others))]
    pltpu.make_async_copy(arrived, arrived, last_rs).wait()
    pltpu.make_async_copy(arrived, arrived, last_ss).wait()
    packed = last_send[...]
    for slot in range(1, len(others) + 1):
        packed = packed + last_recv[slot]

    def value_of(index):
        value = jnp.sum(jnp.where(lane_row // width == index, packed, 0.0), axis=1, keepdims=True)
        return jnp.broadcast_to(value, (1, layers))

    wm, su, sm, sq, zm, zq, am = [value_of(index) for index in range(len(rows))]
    gam_new = gam - 2.0 * a * (dlt + b * su) + a * a * (wm + 2.0 * b * sm + b * b * sq)
    dlt_new = dlt - 2.0 * a * (wm + b * sm) + a * a * (am + 2.0 * b * zm + b * b * zq)
    b_new = gam_new / gam
    a_new = gam_new / (dlt_new - b_new * gam_new / a)
    for i in range(rows_x):
        at = slice(i * rows_y, (i + 1) * rows_y)
        z = nloc_ref[at, :] + (wide[at, :layers] + wide[at, layers:]) + b * z_ref[at, :]
        w = w_ref[at, :] - a * z
        r = r_ref[at, :]
        p = r * inv_ref[at, :] + b_new * p_ref[at, :]
        s = w + b_new * s_ref[at, :]
        x_ref[at, :] = x_ref[at, :] + a_new * p
        r_ref[at, :] = r - a_new * s


def hand_on(x_ref, r_ref, x_out, r_out):
    x_out[...] = x_ref[...]
    r_out[...] = r_ref[...]


def local(
    right_side,
    accumulation,
    trans_x,
    trans_y,
    trans_z,
    perf_cells,
    perf_live,
    well_region,
    schur_blocks,
):
    rows_x, rows_y, layers = right_side.shape
    cols = rows_x * rows_y
    wells, perf = perf_cells.shape
    n, ny = lax.axis_size("gx"), lax.axis_size("gy")
    chunk = WCAP * perf
    f32, bf16, i32 = jnp.float32, jnp.bfloat16, jnp.int32
    vmem, dma = pltpu.VMEM, pltpu.SemaphoreType.DMA
    field = vmem((cols, layers), f32)
    fields = [value.reshape(cols, layers) for value in (right_side, accumulation, trans_x, trans_y, trans_z)]
    in_vmem = pl.BlockSpec(memory_space=pltpu.VMEM)
    outs = pl.pallas_call(
        functools.partial(kernel, n, ny, rows_x, rows_y),
        out_shape=[jax.ShapeDtypeStruct((cols, layers), f32)] * 2,
        in_specs=[pl.BlockSpec(memory_space=pl.ANY)] * 9,
        out_specs=[in_vmem] * 2,
        scratch_shapes=[
            pltpu.SMEM((1, wells), i32),
            vmem((wells, perf), i32),
            vmem((wells, perf), i32),
        ]
        + [field] * 5
        + [
            vmem((wells, perf, perf), f32),
            vmem((n * WCAP, perf, perf), f32),
            vmem((n * WCAP, perf, perf), f32),
            vmem((n * WCAP, 2 * perf, perf), bf16),
            vmem((cols, n * chunk), bf16),
            vmem((2 * layers, n * chunk), bf16),
            vmem((n, 1, chunk), i32),
            vmem((n, 1, chunk), i32),
            vmem((n, 1, chunk), i32),
            vmem((2, n, 1, chunk + layers), f32),
            vmem((2, n, 1, chunk + layers), f32),
            vmem((2, n, 1, chunk), f32),
            vmem((2, n, 1, chunk), f32),
            vmem((2, 1, layers), f32),
            vmem((2, ny, 1, layers), f32),
            vmem((2, 2, rows_x, layers), f32),
            vmem((2, 2, rows_y, layers), f32),
            vmem((2, 2, rows_x, layers), f32),
            vmem((rows_x, layers), f32),
            vmem((rows_y, layers), f32),
            vmem((rows_x, layers), f32),
            vmem((cols + rows_y, layers), f32),
        ]
        + [field] * 11
        + [
            vmem((1, layers), f32),
            vmem((1, layers), f32),
            vmem((n * ny, 1, layers), f32),
            vmem((1, layers), f32),
            dma,
            dma((5,)),
            dma((3,)),
            dma((n,)),
            dma((n,)),
            dma((n,)),
            dma((n,)),
            dma((2,)),
            dma((2,)),
            dma((2, 4)),
            dma((2, 4)),
            dma((2, n)),
            dma((2, n)),
            dma((2, n)),
            dma((2, n)),
            dma((2, ny)),
            dma((2, ny)),
            dma,
            dma,
        ],
        compiler_params=pltpu.CompilerParams(
            collective_id=0, has_side_effects=True, vmem_limit_bytes=60 * 1024 * 1024
        ),
    )(well_region.reshape(1, wells), *fields, perf_cells, perf_live, schur_blocks)
    outs = pl.pallas_call(
        hand_on,
        out_shape=[jax.ShapeDtypeStruct((cols, layers), f32)] * 2,
        in_specs=[in_vmem] * 2,
        out_specs=[in_vmem] * 2,
    )(*outs)
    return tuple(value.reshape(right_side.shape) for value in outs)


def solution(mesh):
    field, rows = P("gx", "gy", None), P(("gx", "gy"), None)
    return jax.shard_map(
        local,
        mesh=mesh,
        in_specs=(field,) * 5 + (rows,) * 3 + (P(("gx", "gy"), None, None),),
        out_specs=(field, field),
        check_vma=False,
    )
```

```python
import functools

import jax
import jax.numpy as jnp
from jax import lax
from jax.experimental import pallas as pl
from jax.experimental.pallas import tpu as pltpu
from jax.sharding import PartitionSpec as P

WCAP = 2
ITERS = 6
NEAR = 1
SEND = ((7, 8), (1, 3), (3, 5), (5, 7), (0, 1))
GAP = 2
PUSH = ((0, 1), (1, 3), (7, 8), (3, 5), (5, 7))
SCATTER = ((0, 3), (3, 5), (5, 8))
MESH = pl.DeviceIdType.MESH


def split_bf16(values):
    high = values.astype(jnp.bfloat16).astype(jnp.float32)
    return high, values - high


def kernel(
    n,
    ny,
    rows_x,
    rows_y,
    region_hbm,
    rhs_hbm,
    acc_hbm,
    tx_hbm,
    ty_hbm,
    tz_hbm,
    cells_hbm,
    live_hbm,
    schur_hbm,
    x_ref,
    r_ref,
    region_ref,
    cells_ref,
    live_ref,
    rhs_ref,
    acc_ref,
    tx_ref,
    ty_ref,
    tz_ref,
    schur_vm,
    schur_out,
    schur_in,
    schur_two,
    onehot,
    vl_ref,
    lay_ref,
    req_send,
    req_recv,
    send_b,
    recv_b,
    send_c,
    recv_c,
    send_g,
    recv_g,
    ysend,
    xrecv,
    yrecv,
    yface_send,
    xface_recv,
    yface_recv,
    fx_ref,
    fy_ref,
    py_ref,
    fz_ref,
    pz_ref,
    inv_ref,
    m_ref,
    w_ref,
    z_ref,
    p_ref,
    s_ref,
    nloc_ref,
    dots_ref,
    last_send,
    last_recv,
    well_dot,
    local_sem,
    field_sem,
    small_sem,
    schur_ss,
    schur_rs,
    req_ss,
    req_rs,
    face_ss,
    face_rs,
    halo_ss,
    halo_rs,
    b_ss,
    b_rs,
    c_ss,
    c_rs,
    g_ss,
    g_rs,
    last_ss,
    last_rs,
):
    cols, layers = rhs_ref.shape
    wells, perf = cells_ref.shape
    chunk = WCAP * perf
    shift = layers.bit_length() - 1
    assert layers == 1 << shift and n == 1 << (n.bit_length() - 1)
    me, my = lax.axis_index("gx"), lax.axis_index("gy")

    def across(d):
        peer = me
        for bit in range(n.bit_length() - 1):
            if d >> bit & 1:
                peer = peer + (1 << bit) * (1 - 2 * lax.rem(lax.div(me, 1 << bit), 2))
        return peer

    def at_peer(d):
        return {"gx": across(d)}

    def at_x(d):
        return {"gx": lax.rem(me + (d + n), n)}

    def at_y(d):
        return {"gy": lax.rem(my + (d + ny), ny)}

    def at_other():
        return {"gy": my + 1 - 2 * lax.rem(my, 2)}

    def at_cross(d):
        return {"gx": across(d), **at_other()}

    near = n * NEAR // 8

    def at_pair(d):
        return at_peer(d) if d < near else at_cross(d)

    def remote(src, dst, ss, rs, where):
        return pltpu.make_async_remote_copy(
            src_ref=src, dst_ref=dst, send_sem=ss, recv_sem=rs, device_id=where, device_id_type=MESH
        )

    schur_copy = pltpu.make_async_copy(schur_hbm, schur_vm, local_sem)
    loads = [
        pltpu.make_async_copy(src, dst, field_sem.at[i])
        for i, (src, dst) in enumerate(
            (
                (ty_hbm, ty_ref),
                (tx_hbm, tx_ref),
                (tz_hbm, tz_ref),
                (acc_hbm, acc_ref),
                (rhs_hbm, rhs_ref),
            )
        )
    ]
    small = [
        pltpu.make_async_copy(src, dst, small_sem.at[i])
        for i, (src, dst) in enumerate(
            ((region_hbm, region_ref), (cells_hbm, cells_ref), (live_hbm, live_ref))
        )
    ]
    for copy in small:
        copy.start()
    barrier = pltpu.get_barrier_semaphore()
    others = [(d, e) for d in range(n - 1, -1, -1) for e in range(ny) if d or e]
    for d, e in others:
        pl.semaphore_signal(barrier, inc=1, device_id={"gx": across(d), **at_y(e)}, device_id_type=MESH)

    for copy in loads:
        copy.start()
    schur_copy.start()
    xrecv[...] = jnp.zeros_like(xrecv)
    for copy in small:
        copy.wait()

    well_at = []
    for d in range(n):
        peer = across(d)
        found = [jnp.int32(0)] * WCAP
        count = jnp.int32(0)
        for w in range(wells):
            match = region_ref[0, w] == peer
            for j in range(WCAP):
                found[j] = jnp.where(jnp.logical_and(match, count == j), jnp.int32(w), found[j])
            count = count + match.astype(jnp.int32)
        well_at.append(found)
        target = req_send if d else req_recv
        for j in range(WCAP):
            used = (count > j).astype(jnp.int32)
            span = slice(j * perf, (j + 1) * perf)
            open_slot = live_ref[pl.ds(found[j], 1), :] * used
            target[d, :, span] = (cells_ref[pl.ds(found[j], 1), :] + 1) * open_slot - 1
    loads[0].wait()
    loads[1].wait()
    yface_send[...] = ty_ref[pl.ds(rows_y - 1, rows_x, stride=rows_y), :]

    pl.semaphore_wait(barrier, len(others))
    requests = [
        remote(req_send.at[d], req_recv.at[d], req_ss.at[d], req_rs.at[d], at_peer(d)) for d in range(1, n)
    ]
    face_out = [
        remote(
            tx_ref.at[pl.ds(cols - rows_y, rows_y)], xface_recv, face_ss.at[0], face_rs.at[0], at_x(1)
        ),
        remote(yface_send, yface_recv, face_ss.at[1], face_rs.at[1], at_y(1)),
    ]
    for copy in requests[::-1] + face_out:
        copy.start()

    def cut(parts):
        return [range(n * low // 8, n * high // 8) for low, high in parts]

    sends, pushes, scatters = cut(SEND), cut(PUSH), cut(SCATTER)
    swaps = [
        remote(
            schur_out.at[pl.ds(d * WCAP, WCAP)],
            schur_in.at[pl.ds(d * WCAP, WCAP)],
            schur_ss.at[d],
            schur_rs.at[d],
            at_other(),
        )
        for d in range(near, n)
    ]
    schur_copy.wait()
    for group in pushes:
        for d in group:
            if d >= near:
                for j in range(WCAP):
                    schur_out[d * WCAP + j] = schur_vm[well_at[d][j]]
                swaps[d - near].start()

    last_x = me == n - 1
    last_y = my == ny - 1
    lane = lax.broadcasted_iota(jnp.int32, (rows_y, layers), 1)
    row = lax.broadcasted_iota(jnp.int32, (rows_y, layers), 0)
    zeros = jnp.zeros((rows_y, layers), jnp.float32)
    column = lax.broadcasted_iota(jnp.int32, (cols, chunk), 0)

    def mark_slots(group):
        for d in group:
            if d:
                requests[d - 1].wait_recv()
            cells = req_recv[d]
            lay_ref[d] = jnp.bitwise_and(cells, layers - 1)
            onehot[:, d * chunk : (d + 1) * chunk] = (
                (column == lax.shift_right_logical(cells, shift)).astype(jnp.float32).astype(jnp.bfloat16)
            )

    mark_slots(range(n * 5 // 8))
    for copy in loads[2:]:
        copy.wait()
    for copy in face_out:
        copy.wait()
    fx_ref[0:rows_y, :] = jnp.where(me == 0, 0.0, xface_recv[...])
    for i in range(rows_x):
        at = slice(i * rows_y, (i + 1) * rows_y)
        after = slice((i + 1) * rows_y, (i + 2) * rows_y)
        fx = tx_ref[at, :]
        if i == rows_x - 1:
            fx = jnp.where(last_x, 0.0, fx)
        fx_ref[after, :] = fx
        fy = ty_ref[at, :]
        below = jnp.where(my == 0, 0.0, yface_recv[i : i + 1, :])
        py = jnp.where(row == 0, below, pltpu.roll(fy, 1, 0))
        fy = jnp.where(jnp.logical_and(last_y, row == rows_y - 1), 0.0, fy)
        fy_ref[at, :] = fy
        py_ref[at, :] = py
        fz = jnp.where(lane == layers - 1, 0.0, tz_ref[at, :])
        pz = pltpu.roll(fz, 1, 1)
        fz_ref[at, :] = fz
        pz_ref[at, :] = pz
        diagonal = acc_ref[at, :] + fx + fx_ref[at, :] + fy + py + fz + pz
        inverse = 1.0 / diagonal
        inv_ref[at, :] = inverse
        r = rhs_ref[at, :]
        r_ref[at, :] = r
        u = r * inverse
        m_ref[at, :] = u
        for ref in (x_ref, w_ref, z_ref, p_ref, s_ref):
            ref[at, :] = zeros
    dots_ref[...] = jnp.zeros_like(dots_ref)

    mark_slots(range(n * 5 // 8, n))
    for copy in requests:
        copy.wait_send()

    layer = lax.broadcasted_iota(jnp.int32, (layers, chunk), 0)
    pick_row = lax.broadcasted_iota(jnp.int32, (16, perf), 0)

    half = layers // 2
    first_half = lax.broadcasted_iota(jnp.int32, (1, layers), 1) < half

    def b_copy(par, d):
        return remote(send_b.at[par, d], recv_b.at[par, d], b_ss.at[par, d], b_rs.at[par, d], at_pair(d))

    def c_copy(par, d):
        return remote(send_c.at[par, d], recv_c.at[par, d], c_ss.at[par, d], c_rs.at[par, d], at_pair(d))

    def g_copy(par, d, slot):
        return remote(send_g.at[par], recv_g.at[par, slot], g_ss.at[par, d], g_rs.at[par, slot], at_y(d))

    def halo_copies(par):
        return [
            remote(
                m_ref.at[pl.ds(cols - rows_y, rows_y)],
                xrecv.at[par, 0],
                halo_ss.at[par, 0],
                halo_rs.at[par, 0],
                at_x(1),
            ),
            remote(
                m_ref.at[pl.ds(0, rows_y)], xrecv.at[par, 1], halo_ss.at[par, 1], halo_rs.at[par, 1], at_x(-1)
            ),
            remote(ysend.at[par, 0], yrecv.at[par, 0], halo_ss.at[par, 2], halo_rs.at[par, 2], at_y(1)),
            remote(ysend.at[par, 1], yrecv.at[par, 1], halo_ss.at[par, 3], halo_rs.at[par, 3], at_y(-1)),
        ]

    def start_sums(par):
        total = recv_b[par, 0, :, chunk:]
        for d in range(1, n):
            total = total + recv_b[par, d, :, chunk:]
        send_g[par] = total
        for d in range(1, ny):
            g_copy(par, d, ny - d).start()
        return total

    def end_sums(par, total):
        for d in range(1, ny):
            g_copy(par, d, d).wait_recv()
            total = total + recv_g[par, d]
        for d in range(1, ny):
            g_copy(par, d, d).wait_send()
        gam = jnp.sum(jnp.where(first_half, total, 0.0), axis=1, keepdims=True)
        dlt = jnp.sum(jnp.where(first_half, 0.0, total), axis=1, keepdims=True)
        return jnp.broadcast_to(gam, (1, layers)), jnp.broadcast_to(dlt, (1, layers))

    def start_halos(par):
        ysend[par, 0] = m_ref[pl.ds(rows_y - 1, rows_x, stride=rows_y), :]
        ysend[par, 1] = m_ref[pl.ds(0, rows_x, stride=rows_y), :]
        halos = halo_copies(par)
        pl.when(me < n - 1)(halos[0].start)
        pl.when(me > 0)(halos[1].start)
        for copy in halos[2:]:
            copy.start()

    def send_field(par):
        high, low = split_bf16(m_ref[...].T)
        lhs = jnp.concatenate([high, low], 0).astype(jnp.bfloat16)
        dots = dots_ref[...]
        for group in sends:
            for d in group:
                part = jnp.dot(
                    lhs, onehot[:, d * chunk : (d + 1) * chunk], preferred_element_type=jnp.float32
                )
                part = part[:layers] + part[layers:]
                picked = jnp.sum(jnp.where(layer == lay_ref[d], part, 0.0), axis=0, keepdims=True)
                target = send_b if d else recv_b
                target[par, d, :, :chunk] = picked
                target[par, d, :, chunk:] = dots
            for d in group:
                if d:
                    b_copy(par, d).start()
            if group is sends[0]:
                start_halos(par)

    def stencil(par):
        halos = halo_copies(par)
        x_up, x_down = halos[:2]

        @pl.when(me < n - 1)
        def _():
            x_up.wait_send()
            x_down.wait_recv()

        @pl.when(me > 0)
        def _():
            x_up.wait_recv()
            x_down.wait_send()

        for copy in halos[2:]:
            copy.wait()
        for i in range(rows_x):
            at = slice(i * rows_y, (i + 1) * rows_y)
            after = slice((i + 1) * rows_y, (i + 2) * rows_y)
            m = m_ref[at, :]
            below = m_ref[(i - 1) * rows_y : i * rows_y, :] if i else xrecv[par, 0]
            above = m_ref[after, :] if i < rows_x - 1 else xrecv[par, 1]
            y_prev = jnp.where(row == 0, yrecv[par, 0, i : i + 1, :], pltpu.roll(m, 1, 0))
            y_next = jnp.where(row == rows_y - 1, yrecv[par, 1, i : i + 1, :], pltpu.roll(m, rows_y - 1, 0))
            nloc_ref[at, :] = (
                acc_ref[at, :] * m
                + fx_ref[after, :] * (m - above)
                + fx_ref[at, :] * (m - below)
                + fy_ref[at, :] * (m - y_next)
                + py_ref[at, :] * (m - y_prev)
                + fz_ref[at, :] * (m - pltpu.roll(m, layers - 1, 1))
                + pz_ref[at, :] * (m - pltpu.roll(m, 1, 1))
            )

    def push(par, keep=False, between=None):
        for index, group in enumerate(pushes):
            if between and index == GAP:
                between()
            for d in group:
                if d:
                    b_copy(par, d).wait_recv()
            for d in group:
                target = send_c if d else recv_c
                for j in range(WCAP):
                    span = slice(j * perf, (j + 1) * perf)
                    high, low = split_bf16(recv_b[par, d, :, span])
                    left = jnp.where(pick_row == 0, high, jnp.where(pick_row == 1, low, 0.0)).astype(
                        jnp.bfloat16
                    )
                    pushed = jnp.dot(
                        jnp.concatenate([left, left], 1),
                        schur_two[d * WCAP + j],
                        preferred_element_type=jnp.float32,
                    )
                    pushed = jnp.sum(pushed, axis=0, keepdims=True)
                    target[par, d, :, span] = pushed
                    if keep:
                        part = recv_b[par, d, :, span] * pushed
                        for low_lane in range(0, perf, layers):
                            well_dot[...] += part[:, low_lane : low_lane + layers]
            for d in group:
                if d:
                    c_copy(par, d).start()

    def scatter(par, group):
        for d in group:
            if d:
                c_copy(par, d).wait_recv()
        for d in group:
            high, low = split_bf16(recv_c[par, d])
            here = layer == lay_ref[d]
            span = slice(d * chunk, (d + 1) * chunk)
            vl_ref[0:layers, span] = jnp.where(here, high, 0.0).astype(jnp.bfloat16)
            vl_ref[layers : 2 * layers, span] = jnp.where(here, low, 0.0).astype(jnp.bfloat16)
        span = slice(group[0] * chunk, (group[-1] + 1) * chunk)
        return lax.dot_general(
            onehot[:, span],
            vl_ref[:, span],
            (((1,), (1,)), ((), ())),
            preferred_element_type=jnp.float32,
        )

    def advance(a, b):
        gamma = jnp.zeros((8, layers), jnp.float32)
        for i in range(rows_x):
            at = slice(i * rows_y, (i + 1) * rows_y)
            inverse = inv_ref[at, :]
            r = r_ref[at, :]
            p = r * inverse + b * p_ref[at, :]
            s = w_ref[at, :] + b * s_ref[at, :]
            p_ref[at, :] = p
            s_ref[at, :] = s
            x_ref[at, :] = x_ref[at, :] + a * p
            r = r - a * s
            r_ref[at, :] = r
            gamma = gamma + jnp.sum((r * r * inverse).reshape(rows_y // 8, 8, layers), axis=0)
        return gamma

    def tiles(values):
        return jnp.sum(values.reshape(rows_y // 8, 8, layers), axis=0)

    def last_copy(d, e):
        slot = d * ny + (ny - e) % ny
        return remote(
            last_send, last_recv.at[slot], last_ss, last_rs, {"gx": across(d), **at_y(e)}
        )

    def step(k, carried):
        gam_old, a_old = carried
        par = lax.rem(k, 2)
        push(par)
        total = start_sums(par)
        stencil(par)
        for group in scatters[:-1]:
            wide = scatter(par, group)
            nloc_ref[...] += wide[:, :layers] + wide[:, layers:]
        for d in range(1, n):
            b_copy(par, d).wait_send()
            c_copy(par, d).wait_send()
        gam, dlt = end_sums(par, total)
        b = jnp.where(k <= 1, 0.0, gam / gam_old)
        a = jnp.where(k == 0, 0.0, jnp.where(k == 1, gam / dlt, gam / (dlt - b * gam / a_old)))
        a_w = jnp.where(k == 0, -1.0, a)
        gamma = advance(a, b)
        wide = scatter(par, scatters[-1])
        delta = jnp.zeros((8, layers), jnp.float32)
        for i in range(rows_x):
            at = slice(i * rows_y, (i + 1) * rows_y)
            z = nloc_ref[at, :] + (wide[at, :layers] + wide[at, layers:]) + b * z_ref[at, :]
            z_ref[at, :] = z
            w = w_ref[at, :] - a_w * z
            w_ref[at, :] = w
            m = w * inv_ref[at, :]
            m_ref[at, :] = m
            delta = delta + jnp.sum((m * r_ref[at, :]).reshape(rows_y // 8, 8, layers), axis=0)
        gamma = jnp.sum(gamma, axis=0, keepdims=True)
        delta = jnp.sum(delta, axis=0, keepdims=True)
        dots_ref[...] = jnp.where(
            first_half, gamma + pltpu.roll(gamma, half, 1), delta + pltpu.roll(delta, half, 1)
        )
        send_field(lax.rem(k + 1, 2))
        return gam, a

    send_field(0)
    for group in pushes:
        for d in group:
            if d >= near:
                swaps[d - near].wait_recv()
            for j in range(WCAP):
                slot = d * WCAP + j
                block = schur_in[slot] if d >= near else schur_vm[well_at[d][j]]
                high = block.astype(jnp.bfloat16)
                schur_two[slot, 0:perf, :] = high
                schur_two[slot, perf : 2 * perf, :] = (block - high.astype(jnp.float32)).astype(jnp.bfloat16)
    for copy in swaps:
        copy.wait_send()

    ones = jnp.ones((1, layers), jnp.float32)
    gam_old, a_old = lax.fori_loop(0, ITERS - 1, step, (ones, ones))

    par = (ITERS - 1) % 2
    zero = jnp.zeros((8, layers), jnp.float32)
    sums = [zero] * 6
    for i in range(rows_x):
        at = slice(i * rows_y, (i + 1) * rows_y)
        inverse, w, s, z, m = inv_ref[at, :], w_ref[at, :], s_ref[at, :], z_ref[at, :], m_ref[at, :]
        q = s * inverse
        terms = (w * m, q * r_ref[at, :], s * m, s * q, z * m, z * q)
        sums = [total + tiles(term) for total, term in zip(sums, terms)]
    well_dot[...] = jnp.zeros_like(well_dot)
    push(par, keep=True, between=lambda: stencil(par))
    image_dot = zero
    for i in range(rows_x):
        at = slice(i * rows_y, (i + 1) * rows_y)
        image_dot = image_dot + tiles(m_ref[at, :] * nloc_ref[at, :])
    rows = [jnp.sum(value, axis=0, keepdims=True) for value in sums + [image_dot]]
    rows[-1] = rows[-1] + well_dot[...]
    values = len(rows) + 1
    width = layers // values
    lane_row = lax.broadcasted_iota(jnp.int32, (1, layers), 1)
    packed = jnp.zeros((1, layers), jnp.float32)
    for index, value in enumerate(rows):
        fold = half
        while fold >= width:
            value = value + pltpu.roll(value, fold, 1)
            fold //= 2
        packed = jnp.where(lane_row // width == index, value, packed)
    last_send[...] = packed
    for d, e in others:
        last_copy(d, e).start()
    total = start_sums(par)
    for group in scatters[:-1]:
        wide = scatter(par, group)
        nloc_ref[...] += wide[:, :layers] + wide[:, layers:]
    for d in range(1, n):
        b_copy(par, d).wait_send()
        c_copy(par, d).wait_send()
    gam, dlt = end_sums(par, total)
    b = gam / gam_old
    a = gam / (dlt - b * gam / a_old)
    advance(a, b)
    wide = scatter(par, scatters[-1])
    arrived = last_recv.at[pl.ds(1, len(others))]
    pltpu.make_async_copy(arrived, arrived, last_rs).wait()
    pltpu.make_async_copy(arrived, arrived, last_ss).wait()
    packed = last_send[...]
    for slot in range(1, len(others) + 1):
        packed = packed + last_recv[slot]

    def value_of(index):
        value = jnp.sum(jnp.where(lane_row // width == index, packed, 0.0), axis=1, keepdims=True)
        return jnp.broadcast_to(value, (1, layers))

    wm, su, sm, sq, zm, zq, am = [value_of(index) for index in range(len(rows))]
    gam_new = gam - 2.0 * a * (dlt + b * su) + a * a * (wm + 2.0 * b * sm + b * b * sq)
    dlt_new = dlt - 2.0 * a * (wm + b * sm) + a * a * (am + 2.0 * b * zm + b * b * zq)
    b_new = gam_new / gam
    a_new = gam_new / (dlt_new - b_new * gam_new / a)
    for i in range(rows_x):
        at = slice(i * rows_y, (i + 1) * rows_y)
        z = nloc_ref[at, :] + (wide[at, :layers] + wide[at, layers:]) + b * z_ref[at, :]
        w = w_ref[at, :] - a * z
        r = r_ref[at, :]
        p = r * inv_ref[at, :] + b_new * p_ref[at, :]
        s = w + b_new * s_ref[at, :]
        x_ref[at, :] = x_ref[at, :] + a_new * p
        r_ref[at, :] = r - a_new * s


def hand_on(x_ref, r_ref, x_out, r_out):
    x_out[...] = x_ref[...]
    r_out[...] = r_ref[...]


def local(
    right_side,
    accumulation,
    trans_x,
    trans_y,
    trans_z,
    perf_cells,
    perf_live,
    well_region,
    schur_blocks,
):
    rows_x, rows_y, layers = right_side.shape
    cols = rows_x * rows_y
    wells, perf = perf_cells.shape
    n, ny = lax.axis_size("gx"), lax.axis_size("gy")
    chunk = WCAP * perf
    f32, bf16, i32 = jnp.float32, jnp.bfloat16, jnp.int32
    vmem, dma = pltpu.VMEM, pltpu.SemaphoreType.DMA
    field = vmem((cols, layers), f32)
    fields = [value.reshape(cols, layers) for value in (right_side, accumulation, trans_x, trans_y, trans_z)]
    in_vmem = pl.BlockSpec(memory_space=pltpu.VMEM)
    outs = pl.pallas_call(
        functools.partial(kernel, n, ny, rows_x, rows_y),
        out_shape=[jax.ShapeDtypeStruct((cols, layers), f32)] * 2,
        in_specs=[pl.BlockSpec(memory_space=pl.ANY)] * 9,
        out_specs=[in_vmem] * 2,
        scratch_shapes=[
            pltpu.SMEM((1, wells), i32),
            vmem((wells, perf), i32),
            vmem((wells, perf), i32),
        ]
        + [field] * 5
        + [
            vmem((wells, perf, perf), f32),
            vmem((n * WCAP, perf, perf), f32),
            vmem((n * WCAP, perf, perf), f32),
            vmem((n * WCAP, 2 * perf, perf), bf16),
            vmem((cols, n * chunk), bf16),
            vmem((2 * layers, n * chunk), bf16),
            vmem((n, 1, chunk), i32),
            vmem((n, 1, chunk), i32),
            vmem((n, 1, chunk), i32),
            vmem((2, n, 1, chunk + layers), f32),
            vmem((2, n, 1, chunk + layers), f32),
            vmem((2, n, 1, chunk), f32),
            vmem((2, n, 1, chunk), f32),
            vmem((2, 1, layers), f32),
            vmem((2, ny, 1, layers), f32),
            vmem((2, 2, rows_x, layers), f32),
            vmem((2, 2, rows_y, layers), f32),
            vmem((2, 2, rows_x, layers), f32),
            vmem((rows_x, layers), f32),
            vmem((rows_y, layers), f32),
            vmem((rows_x, layers), f32),
            vmem((cols + rows_y, layers), f32),
        ]
        + [field] * 11
        + [
            vmem((1, layers), f32),
            vmem((1, layers), f32),
            vmem((n * ny, 1, layers), f32),
            vmem((1, layers), f32),
            dma,
            dma((5,)),
            dma((3,)),
            dma((n,)),
            dma((n,)),
            dma((n,)),
            dma((n,)),
            dma((2,)),
            dma((2,)),
            dma((2, 4)),
            dma((2, 4)),
            dma((2, n)),
            dma((2, n)),
            dma((2, n)),
            dma((2, n)),
            dma((2, ny)),
            dma((2, ny)),
            dma,
            dma,
        ],
        compiler_params=pltpu.CompilerParams(
            collective_id=0, has_side_effects=True, vmem_limit_bytes=60 * 1024 * 1024
        ),
    )(well_region.reshape(1, wells), *fields, perf_cells, perf_live, schur_blocks)
    outs = pl.pallas_call(
        hand_on,
        out_shape=[jax.ShapeDtypeStruct((cols, layers), f32)] * 2,
        in_specs=[in_vmem] * 2,
        out_specs=[in_vmem] * 2,
    )(*outs)
    return tuple(value.reshape(right_side.shape) for value in outs)


def solution(mesh):
    field, rows = P("gx", "gy", None), P(("gx", "gy"), None)
    return jax.shard_map(
        local,
        mesh=mesh,
        in_specs=(field,) * 5 + (rows,) * 3 + (P(("gx", "gy"), None, None),),
        out_specs=(field, field),
        check_vma=False,
    )
```

```python
import functools

import jax
import jax.numpy as jnp
from jax import lax
from jax.experimental import pallas as pl
from jax.experimental.pallas import tpu as pltpu
from jax.sharding import PartitionSpec as P

WCAP = 2
ITERS = 6
NEAR = 1
SEND = ((7, 8), (1, 3), (3, 5), (5, 7), (0, 1))
GAP = 2
PUSH = ((0, 1), (1, 3), (7, 8), (3, 5), (5, 7))
SCATTER = ((0, 1), (1, 3), (3, 5), (5, 8))
MESH = pl.DeviceIdType.MESH


def split_bf16(values):
    high = values.astype(jnp.bfloat16).astype(jnp.float32)
    return high, values - high


def kernel(
    n,
    ny,
    rows_x,
    rows_y,
    region_hbm,
    rhs_hbm,
    acc_hbm,
    tx_hbm,
    ty_hbm,
    tz_hbm,
    cells_hbm,
    live_hbm,
    schur_hbm,
    x_ref,
    r_ref,
    region_ref,
    cells_ref,
    live_ref,
    rhs_ref,
    acc_ref,
    tx_ref,
    ty_ref,
    tz_ref,
    schur_vm,
    schur_out,
    schur_in,
    schur_two,
    onehot,
    vl_ref,
    lay_ref,
    req_send,
    req_recv,
    send_b,
    recv_b,
    send_c,
    recv_c,
    send_g,
    recv_g,
    ysend,
    xrecv,
    yrecv,
    yface_send,
    xface_recv,
    yface_recv,
    fx_ref,
    fy_ref,
    py_ref,
    fz_ref,
    pz_ref,
    inv_ref,
    m_ref,
    w_ref,
    z_ref,
    p_ref,
    s_ref,
    nloc_ref,
    dots_ref,
    last_send,
    last_recv,
    well_dot,
    local_sem,
    field_sem,
    small_sem,
    schur_ss,
    schur_rs,
    req_ss,
    req_rs,
    face_ss,
    face_rs,
    halo_ss,
    halo_rs,
    b_ss,
    b_rs,
    c_ss,
    c_rs,
    g_ss,
    g_rs,
    last_ss,
    last_rs,
):
    cols, layers = rhs_ref.shape
    wells, perf = cells_ref.shape
    chunk = WCAP * perf
    shift = layers.bit_length() - 1
    assert layers == 1 << shift and n == 1 << (n.bit_length() - 1)
    me, my = lax.axis_index("gx"), lax.axis_index("gy")

    def across(d):
        peer = me
        for bit in range(n.bit_length() - 1):
            if d >> bit & 1:
                peer = peer + (1 << bit) * (1 - 2 * lax.rem(lax.div(me, 1 << bit), 2))
        return peer

    def at_peer(d):
        return {"gx": across(d)}

    def at_x(d):
        return {"gx": lax.rem(me + (d + n), n)}

    def at_y(d):
        return {"gy": lax.rem(my + (d + ny), ny)}

    def at_other():
        return {"gy": my + 1 - 2 * lax.rem(my, 2)}

    def at_cross(d):
        return {"gx": across(d), **at_other()}

    near = n * NEAR // 8

    def at_pair(d):
        return at_peer(d) if d < near else at_cross(d)

    def remote(src, dst, ss, rs, where):
        return pltpu.make_async_remote_copy(
            src_ref=src, dst_ref=dst, send_sem=ss, recv_sem=rs, device_id=where, device_id_type=MESH
        )

    schur_copy = pltpu.make_async_copy(schur_hbm, schur_vm, local_sem)
    loads = [
        pltpu.make_async_copy(src, dst, field_sem.at[i])
        for i, (src, dst) in enumerate(
            (
                (ty_hbm, ty_ref),
                (tx_hbm, tx_ref),
                (tz_hbm, tz_ref),
                (acc_hbm, acc_ref),
                (rhs_hbm, rhs_ref),
            )
        )
    ]
    small = [
        pltpu.make_async_copy(src, dst, small_sem.at[i])
        for i, (src, dst) in enumerate(
            ((region_hbm, region_ref), (cells_hbm, cells_ref), (live_hbm, live_ref))
        )
    ]
    for copy in small:
        copy.start()
    barrier = pltpu.get_barrier_semaphore()
    others = [(d, e) for d in range(n - 1, -1, -1) for e in range(ny) if d or e]
    for d, e in others:
        pl.semaphore_signal(barrier, inc=1, device_id={"gx": across(d), **at_y(e)}, device_id_type=MESH)

    for copy in loads:
        copy.start()
    schur_copy.start()
    xrecv[...] = jnp.zeros_like(xrecv)
    for copy in small:
        copy.wait()

    well_at = []
    for d in range(n):
        peer = across(d)
        found = [jnp.int32(0)] * WCAP
        count = jnp.int32(0)
        for w in range(wells):
            match = region_ref[0, w] == peer
            for j in range(WCAP):
                found[j] = jnp.where(jnp.logical_and(match, count == j), jnp.int32(w), found[j])
            count = count + match.astype(jnp.int32)
        well_at.append(found)
        target = req_send if d else req_recv
        for j in range(WCAP):
            used = (count > j).astype(jnp.int32)
            span = slice(j * perf, (j + 1) * perf)
            open_slot = live_ref[pl.ds(found[j], 1), :] * used
            target[d, :, span] = (cells_ref[pl.ds(found[j], 1), :] + 1) * open_slot - 1
    loads[0].wait()
    loads[1].wait()
    yface_send[...] = ty_ref[pl.ds(rows_y - 1, rows_x, stride=rows_y), :]

    pl.semaphore_wait(barrier, len(others))
    requests = [
        remote(req_send.at[d], req_recv.at[d], req_ss.at[d], req_rs.at[d], at_peer(d)) for d in range(1, n)
    ]
    face_out = [
        remote(
            tx_ref.at[pl.ds(cols - rows_y, rows_y)], xface_recv, face_ss.at[0], face_rs.at[0], at_x(1)
        ),
        remote(yface_send, yface_recv, face_ss.at[1], face_rs.at[1], at_y(1)),
    ]
    for copy in requests[::-1] + face_out:
        copy.start()

    def cut(parts):
        return [range(n * low // 8, n * high // 8) for low, high in parts]

    sends, pushes, scatters = cut(SEND), cut(PUSH), cut(SCATTER)
    swaps = [
        remote(
            schur_out.at[pl.ds(d * WCAP, WCAP)],
            schur_in.at[pl.ds(d * WCAP, WCAP)],
            schur_ss.at[d],
            schur_rs.at[d],
            at_other(),
        )
        for d in range(near, n)
    ]
    schur_copy.wait()
    for group in pushes:
        for d in group:
            if d >= near:
                for j in range(WCAP):
                    schur_out[d * WCAP + j] = schur_vm[well_at[d][j]]
                swaps[d - near].start()

    last_x = me == n - 1
    last_y = my == ny - 1
    lane = lax.broadcasted_iota(jnp.int32, (rows_y, layers), 1)
    row = lax.broadcasted_iota(jnp.int32, (rows_y, layers), 0)
    zeros = jnp.zeros((rows_y, layers), jnp.float32)
    column = lax.broadcasted_iota(jnp.int32, (cols, chunk), 0)

    def mark_slots(group):
        for d in group:
            if d:
                requests[d - 1].wait_recv()
            cells = req_recv[d]
            lay_ref[d] = jnp.bitwise_and(cells, layers - 1)
            onehot[:, d * chunk : (d + 1) * chunk] = (
                (column == lax.shift_right_logical(cells, shift)).astype(jnp.float32).astype(jnp.bfloat16)
            )

    mark_slots(range(n * 5 // 8))
    for copy in loads[2:]:
        copy.wait()
    for copy in face_out:
        copy.wait()
    fx_ref[0:rows_y, :] = jnp.where(me == 0, 0.0, xface_recv[...])
    for i in range(rows_x):
        at = slice(i * rows_y, (i + 1) * rows_y)
        after = slice((i + 1) * rows_y, (i + 2) * rows_y)
        fx = tx_ref[at, :]
        if i == rows_x - 1:
            fx = jnp.where(last_x, 0.0, fx)
        fx_ref[after, :] = fx
        fy = ty_ref[at, :]
        below = jnp.where(my == 0, 0.0, yface_recv[i : i + 1, :])
        py = jnp.where(row == 0, below, pltpu.roll(fy, 1, 0))
        fy = jnp.where(jnp.logical_and(last_y, row == rows_y - 1), 0.0, fy)
        fy_ref[at, :] = fy
        py_ref[at, :] = py
        fz = jnp.where(lane == layers - 1, 0.0, tz_ref[at, :])
        pz = pltpu.roll(fz, 1, 1)
        fz_ref[at, :] = fz
        pz_ref[at, :] = pz
        diagonal = acc_ref[at, :] + fx + fx_ref[at, :] + fy + py + fz + pz
        inverse = 1.0 / diagonal
        inv_ref[at, :] = inverse
        r = rhs_ref[at, :]
        r_ref[at, :] = r
        u = r * inverse
        m_ref[at, :] = u
        for ref in (x_ref, w_ref, z_ref, p_ref, s_ref):
            ref[at, :] = zeros
    dots_ref[...] = jnp.zeros_like(dots_ref)

    mark_slots(range(n * 5 // 8, n))
    for copy in requests:
        copy.wait_send()

    layer = lax.broadcasted_iota(jnp.int32, (layers, chunk), 0)
    pick_row = lax.broadcasted_iota(jnp.int32, (16, perf), 0)

    half = layers // 2
    first_half = lax.broadcasted_iota(jnp.int32, (1, layers), 1) < half

    def b_copy(par, d):
        return remote(send_b.at[par, d], recv_b.at[par, d], b_ss.at[par, d], b_rs.at[par, d], at_pair(d))

    def c_copy(par, d):
        return remote(send_c.at[par, d], recv_c.at[par, d], c_ss.at[par, d], c_rs.at[par, d], at_pair(d))

    def g_copy(par, d, slot):
        return remote(send_g.at[par], recv_g.at[par, slot], g_ss.at[par, d], g_rs.at[par, slot], at_y(d))

    def halo_copies(par):
        return [
            remote(
                m_ref.at[pl.ds(cols - rows_y, rows_y)],
                xrecv.at[par, 0],
                halo_ss.at[par, 0],
                halo_rs.at[par, 0],
                at_x(1),
            ),
            remote(
                m_ref.at[pl.ds(0, rows_y)], xrecv.at[par, 1], halo_ss.at[par, 1], halo_rs.at[par, 1], at_x(-1)
            ),
            remote(ysend.at[par, 0], yrecv.at[par, 0], halo_ss.at[par, 2], halo_rs.at[par, 2], at_y(1)),
            remote(ysend.at[par, 1], yrecv.at[par, 1], halo_ss.at[par, 3], halo_rs.at[par, 3], at_y(-1)),
        ]

    def start_sums(par):
        total = recv_b[par, 0, :, chunk:]
        for d in range(1, n):
            total = total + recv_b[par, d, :, chunk:]
        send_g[par] = total
        for d in range(1, ny):
            g_copy(par, d, ny - d).start()
        return total

    def end_sums(par, total):
        for d in range(1, ny):
            g_copy(par, d, d).wait_recv()
            total = total + recv_g[par, d]
        for d in range(1, ny):
            g_copy(par, d, d).wait_send()
        gam = jnp.sum(jnp.where(first_half, total, 0.0), axis=1, keepdims=True)
        dlt = jnp.sum(jnp.where(first_half, 0.0, total), axis=1, keepdims=True)
        return jnp.broadcast_to(gam, (1, layers)), jnp.broadcast_to(dlt, (1, layers))

    def start_halos(par):
        ysend[par, 0] = m_ref[pl.ds(rows_y - 1, rows_x, stride=rows_y), :]
        ysend[par, 1] = m_ref[pl.ds(0, rows_x, stride=rows_y), :]
        halos = halo_copies(par)
        pl.when(me < n - 1)(halos[0].start)
        pl.when(me > 0)(halos[1].start)
        for copy in halos[2:]:
            copy.start()

    def send_field(par):
        high, low = split_bf16(m_ref[...].T)
        lhs = jnp.concatenate([high, low], 0).astype(jnp.bfloat16)
        dots = dots_ref[...]
        for group in sends:
            for d in group:
                part = jnp.dot(
                    lhs, onehot[:, d * chunk : (d + 1) * chunk], preferred_element_type=jnp.float32
                )
                part = part[:layers] + part[layers:]
                picked = jnp.sum(jnp.where(layer == lay_ref[d], part, 0.0), axis=0, keepdims=True)
                target = send_b if d else recv_b
                target[par, d, :, :chunk] = picked
                target[par, d, :, chunk:] = dots
            for d in group:
                if d:
                    b_copy(par, d).start()
            if group is sends[0]:
                start_halos(par)

    def stencil(par):
        halos = halo_copies(par)
        x_up, x_down = halos[:2]

        @pl.when(me < n - 1)
        def _():
            x_up.wait_send()
            x_down.wait_recv()

        @pl.when(me > 0)
        def _():
            x_up.wait_recv()
            x_down.wait_send()

        for copy in halos[2:]:
            copy.wait()
        for i in range(rows_x):
            at = slice(i * rows_y, (i + 1) * rows_y)
            after = slice((i + 1) * rows_y, (i + 2) * rows_y)
            m = m_ref[at, :]
            below = m_ref[(i - 1) * rows_y : i * rows_y, :] if i else xrecv[par, 0]
            above = m_ref[after, :] if i < rows_x - 1 else xrecv[par, 1]
            y_prev = jnp.where(row == 0, yrecv[par, 0, i : i + 1, :], pltpu.roll(m, 1, 0))
            y_next = jnp.where(row == rows_y - 1, yrecv[par, 1, i : i + 1, :], pltpu.roll(m, rows_y - 1, 0))
            nloc_ref[at, :] = (
                acc_ref[at, :] * m
                + fx_ref[after, :] * (m - above)
                + fx_ref[at, :] * (m - below)
                + fy_ref[at, :] * (m - y_next)
                + py_ref[at, :] * (m - y_prev)
                + fz_ref[at, :] * (m - pltpu.roll(m, layers - 1, 1))
                + pz_ref[at, :] * (m - pltpu.roll(m, 1, 1))
            )

    def push(par, keep=False, between=None):
        for index, group in enumerate(pushes):
            if between and index == GAP:
                between()
            for d in group:
                if d:
                    b_copy(par, d).wait_recv()
            for d in group:
                target = send_c if d else recv_c
                for j in range(WCAP):
                    span = slice(j * perf, (j + 1) * perf)
                    high, low = split_bf16(recv_b[par, d, :, span])
                    left = jnp.where(pick_row == 0, high, jnp.where(pick_row == 1, low, 0.0)).astype(
                        jnp.bfloat16
                    )
                    pushed = jnp.dot(
                        jnp.concatenate([left, left], 1),
                        schur_two[d * WCAP + j],
                        preferred_element_type=jnp.float32,
                    )
                    pushed = jnp.sum(pushed, axis=0, keepdims=True)
                    target[par, d, :, span] = pushed
                    if keep:
                        part = recv_b[par, d, :, span] * pushed
                        for low_lane in range(0, perf, layers):
                            well_dot[...] += part[:, low_lane : low_lane + layers]
            for d in group:
                if d:
                    c_copy(par, d).start()

    def scatter(par, group):
        for d in group:
            if d:
                c_copy(par, d).wait_recv()
        for d in group:
            high, low = split_bf16(recv_c[par, d])
            here = layer == lay_ref[d]
            span = slice(d * chunk, (d + 1) * chunk)
            vl_ref[0:layers, span] = jnp.where(here, high, 0.0).astype(jnp.bfloat16)
            vl_ref[layers : 2 * layers, span] = jnp.where(here, low, 0.0).astype(jnp.bfloat16)
        span = slice(group[0] * chunk, (group[-1] + 1) * chunk)
        return lax.dot_general(
            onehot[:, span],
            vl_ref[:, span],
            (((1,), (1,)), ((), ())),
            preferred_element_type=jnp.float32,
        )

    def advance(a, b):
        gamma = jnp.zeros((8, layers), jnp.float32)
        for i in range(rows_x):
            at = slice(i * rows_y, (i + 1) * rows_y)
            inverse = inv_ref[at, :]
            r = r_ref[at, :]
            p = r * inverse + b * p_ref[at, :]
            s = w_ref[at, :] + b * s_ref[at, :]
            p_ref[at, :] = p
            s_ref[at, :] = s
            x_ref[at, :] = x_ref[at, :] + a * p
            r = r - a * s
            r_ref[at, :] = r
            gamma = gamma + jnp.sum((r * r * inverse).reshape(rows_y // 8, 8, layers), axis=0)
        return gamma

    def tiles(values):
        return jnp.sum(values.reshape(rows_y // 8, 8, layers), axis=0)

    def last_copy(d, e):
        slot = d * ny + (ny - e) % ny
        return remote(
            last_send, last_recv.at[slot], last_ss, last_rs, {"gx": across(d), **at_y(e)}
        )

    def step(k, carried):
        gam_old, a_old = carried
        par = lax.rem(k, 2)
        push(par)
        total = start_sums(par)
        stencil(par)
        for group in scatters[:-1]:
            wide = scatter(par, group)
            nloc_ref[...] += wide[:, :layers] + wide[:, layers:]
        for d in range(1, n):
            b_copy(par, d).wait_send()
            c_copy(par, d).wait_send()
        gam, dlt = end_sums(par, total)
        b = jnp.where(k <= 1, 0.0, gam / gam_old)
        a = jnp.where(k == 0, 0.0, jnp.where(k == 1, gam / dlt, gam / (dlt - b * gam / a_old)))
        a_w = jnp.where(k == 0, -1.0, a)
        gamma = advance(a, b)
        wide = scatter(par, scatters[-1])
        delta = jnp.zeros((8, layers), jnp.float32)
        for i in range(rows_x):
            at = slice(i * rows_y, (i + 1) * rows_y)
            z = nloc_ref[at, :] + (wide[at, :layers] + wide[at, layers:]) + b * z_ref[at, :]
            z_ref[at, :] = z
            w = w_ref[at, :] - a_w * z
            w_ref[at, :] = w
            m = w * inv_ref[at, :]
            m_ref[at, :] = m
            delta = delta + jnp.sum((m * r_ref[at, :]).reshape(rows_y // 8, 8, layers), axis=0)
        gamma = jnp.sum(gamma, axis=0, keepdims=True)
        delta = jnp.sum(delta, axis=0, keepdims=True)
        dots_ref[...] = jnp.where(
            first_half, gamma + pltpu.roll(gamma, half, 1), delta + pltpu.roll(delta, half, 1)
        )
        send_field(lax.rem(k + 1, 2))
        return gam, a

    send_field(0)
    for group in pushes:
        for d in group:
            if d >= near:
                swaps[d - near].wait_recv()
            for j in range(WCAP):
                slot = d * WCAP + j
                block = schur_in[slot] if d >= near else schur_vm[well_at[d][j]]
                high = block.astype(jnp.bfloat16)
                schur_two[slot, 0:perf, :] = high
                schur_two[slot, perf : 2 * perf, :] = (block - high.astype(jnp.float32)).astype(jnp.bfloat16)
    for copy in swaps:
        copy.wait_send()

    ones = jnp.ones((1, layers), jnp.float32)
    gam_old, a_old = lax.fori_loop(0, ITERS - 1, step, (ones, ones))

    par = (ITERS - 1) % 2
    zero = jnp.zeros((8, layers), jnp.float32)
    sums = [zero] * 6
    for i in range(rows_x):
        at = slice(i * rows_y, (i + 1) * rows_y)
        inverse, w, s, z, m = inv_ref[at, :], w_ref[at, :], s_ref[at, :], z_ref[at, :], m_ref[at, :]
        q = s * inverse
        terms = (w * m, q * r_ref[at, :], s * m, s * q, z * m, z * q)
        sums = [total + tiles(term) for total, term in zip(sums, terms)]
    well_dot[...] = jnp.zeros_like(well_dot)
    push(par, keep=True, between=lambda: stencil(par))
    image_dot = zero
    for i in range(rows_x):
        at = slice(i * rows_y, (i + 1) * rows_y)
        image_dot = image_dot + tiles(m_ref[at, :] * nloc_ref[at, :])
    rows = [jnp.sum(value, axis=0, keepdims=True) for value in sums + [image_dot]]
    rows[-1] = rows[-1] + well_dot[...]
    values = len(rows) + 1
    width = layers // values
    lane_row = lax.broadcasted_iota(jnp.int32, (1, layers), 1)
    packed = jnp.zeros((1, layers), jnp.float32)
    for index, value in enumerate(rows):
        fold = half
        while fold >= width:
            value = value + pltpu.roll(value, fold, 1)
            fold //= 2
        packed = jnp.where(lane_row // width == index, value, packed)
    last_send[...] = packed
    for d, e in others:
        last_copy(d, e).start()
    total = start_sums(par)
    for group in scatters[:-1]:
        wide = scatter(par, group)
        nloc_ref[...] += wide[:, :layers] + wide[:, layers:]
    for d in range(1, n):
        b_copy(par, d).wait_send()
        c_copy(par, d).wait_send()
    gam, dlt = end_sums(par, total)
    b = gam / gam_old
    a = gam / (dlt - b * gam / a_old)
    advance(a, b)
    wide = scatter(par, scatters[-1])
    arrived = last_recv.at[pl.ds(1, len(others))]
    pltpu.make_async_copy(arrived, arrived, last_rs).wait()
    pltpu.make_async_copy(arrived, arrived, last_ss).wait()
    packed = last_send[...]
    for slot in range(1, len(others) + 1):
        packed = packed + last_recv[slot]

    def value_of(index):
        value = jnp.sum(jnp.where(lane_row // width == index, packed, 0.0), axis=1, keepdims=True)
        return jnp.broadcast_to(value, (1, layers))

    wm, su, sm, sq, zm, zq, am = [value_of(index) for index in range(len(rows))]
    gam_new = gam - 2.0 * a * (dlt + b * su) + a * a * (wm + 2.0 * b * sm + b * b * sq)
    dlt_new = dlt - 2.0 * a * (wm + b * sm) + a * a * (am + 2.0 * b * zm + b * b * zq)
    b_new = gam_new / gam
    a_new = gam_new / (dlt_new - b_new * gam_new / a)
    for i in range(rows_x):
        at = slice(i * rows_y, (i + 1) * rows_y)
        z = nloc_ref[at, :] + (wide[at, :layers] + wide[at, layers:]) + b * z_ref[at, :]
        w = w_ref[at, :] - a * z
        r = r_ref[at, :]
        p = r * inv_ref[at, :] + b_new * p_ref[at, :]
        s = w + b_new * s_ref[at, :]
        x_ref[at, :] = x_ref[at, :] + a_new * p
        r_ref[at, :] = r - a_new * s


def hand_on(x_ref, r_ref, x_out, r_out):
    x_out[...] = x_ref[...]
    r_out[...] = r_ref[...]


def local(
    right_side,
    accumulation,
    trans_x,
    trans_y,
    trans_z,
    perf_cells,
    perf_live,
    well_region,
    schur_blocks,
):
    rows_x, rows_y, layers = right_side.shape
    cols = rows_x * rows_y
    wells, perf = perf_cells.shape
    n, ny = lax.axis_size("gx"), lax.axis_size("gy")
    chunk = WCAP * perf
    f32, bf16, i32 = jnp.float32, jnp.bfloat16, jnp.int32
    vmem, dma = pltpu.VMEM, pltpu.SemaphoreType.DMA
    field = vmem((cols, layers), f32)
    fields = [value.reshape(cols, layers) for value in (right_side, accumulation, trans_x, trans_y, trans_z)]
    in_vmem = pl.BlockSpec(memory_space=pltpu.VMEM)
    outs = pl.pallas_call(
        functools.partial(kernel, n, ny, rows_x, rows_y),
        out_shape=[jax.ShapeDtypeStruct((cols, layers), f32)] * 2,
        in_specs=[pl.BlockSpec(memory_space=pl.ANY)] * 9,
        out_specs=[in_vmem] * 2,
        scratch_shapes=[
            pltpu.SMEM((1, wells), i32),
            vmem((wells, perf), i32),
            vmem((wells, perf), i32),
        ]
        + [field] * 5
        + [
            vmem((wells, perf, perf), f32),
            vmem((n * WCAP, perf, perf), f32),
            vmem((n * WCAP, perf, perf), f32),
            vmem((n * WCAP, 2 * perf, perf), bf16),
            vmem((cols, n * chunk), bf16),
            vmem((2 * layers, n * chunk), bf16),
            vmem((n, 1, chunk), i32),
            vmem((n, 1, chunk), i32),
            vmem((n, 1, chunk), i32),
            vmem((2, n, 1, chunk + layers), f32),
            vmem((2, n, 1, chunk + layers), f32),
            vmem((2, n, 1, chunk), f32),
            vmem((2, n, 1, chunk), f32),
            vmem((2, 1, layers), f32),
            vmem((2, ny, 1, layers), f32),
            vmem((2, 2, rows_x, layers), f32),
            vmem((2, 2, rows_y, layers), f32),
            vmem((2, 2, rows_x, layers), f32),
            vmem((rows_x, layers), f32),
            vmem((rows_y, layers), f32),
            vmem((rows_x, layers), f32),
            vmem((cols + rows_y, layers), f32),
        ]
        + [field] * 11
        + [
            vmem((1, layers), f32),
            vmem((1, layers), f32),
            vmem((n * ny, 1, layers), f32),
            vmem((1, layers), f32),
            dma,
            dma((5,)),
            dma((3,)),
            dma((n,)),
            dma((n,)),
            dma((n,)),
            dma((n,)),
            dma((2,)),
            dma((2,)),
            dma((2, 4)),
            dma((2, 4)),
            dma((2, n)),
            dma((2, n)),
            dma((2, n)),
            dma((2, n)),
            dma((2, ny)),
            dma((2, ny)),
            dma,
            dma,
        ],
        compiler_params=pltpu.CompilerParams(
            collective_id=0, has_side_effects=True, vmem_limit_bytes=60 * 1024 * 1024
        ),
    )(well_region.reshape(1, wells), *fields, perf_cells, perf_live, schur_blocks)
    outs = pl.pallas_call(
        hand_on,
        out_shape=[jax.ShapeDtypeStruct((cols, layers), f32)] * 2,
        in_specs=[in_vmem] * 2,
        out_specs=[in_vmem] * 2,
    )(*outs)
    return tuple(value.reshape(right_side.shape) for value in outs)


def solution(mesh):
    field, rows = P("gx", "gy", None), P(("gx", "gy"), None)
    return jax.shard_map(
        local,
        mesh=mesh,
        in_specs=(field,) * 5 + (rows,) * 3 + (P(("gx", "gy"), None, None),),
        out_specs=(field, field),
        check_vma=False,
    )
```
